256 devices in a mesh: segment: 4 (over z_hi, core), expert: 64 (over z_lo, x, y).
Axes of the slice: x: 4, y: 4, z: 8 (z_hi: 2, z_lo: 4; z = z_hi * 4 + z_lo), core: 2. Of those that a mesh axis runs over, the one named last changes fastest.
Arguments:
- act_a: bfloat16 [4, 1536, 2048], P('segment', 'expert'), may hold values from -6 to 6
- route_a1: int32 [4, 1536, 8], P('segment', 'expert'), may hold values from 0 to 63, all different within a row; in each aligned block of 24 rows (0 to 23, 24 to 47, ..., all dimensions but the last counted through in order) at most 4 rows name the same one
- gate_a1: float32 [4, 1536, 8], P('segment', 'expert'), may hold values from 0.1 to 0.5
- act_b1: bfloat16 [4, 1536, 2048], P('segment', 'expert'), may hold values from -6 to 6
- route_b1: int32 [4, 1536, 8], P('segment', 'expert'), may hold values from 0 to 63, all different within a row; in each aligned block of 24 rows (0 to 23, 24 to 47, ..., all dimensions but the last counted through in order) at most 4 rows name the same one
- gate_b1: float32 [4, 1536, 8], P('segment', 'expert'), may hold values from 0.1 to 0.5
- grad_b1: bfloat16 [4, 1536, 2048], P('segment', 'expert'), may hold values from -6 to 6
- act_b2: bfloat16 [4, 1536, 2048], P('segment', 'expert'), may hold values from -6 to 6
- route_a2: int32 [4, 1536, 8], P('segment', 'expert'), may hold values from 0 to 63, all different within a row; in each aligned block of 24 rows (0 to 23, 24 to 47, ..., all dimensions but the last counted through in order) at most 4 rows name the same one
- gate_a2: float32 [4, 1536, 8], P('segment', 'expert'), may hold values from 0.1 to 0.5
- route_b2: int32 [4, 1536, 8], P('segment', 'expert'), may hold values from 0 to 63, all different within a row; in each aligned block of 24 rows (0 to 23, 24 to 47, ..., all dimensions but the last counted through in order) at most 4 rows name the same one
- gate_b2: float32 [4, 1536, 8], P('segment', 'expert'), may hold values from 0.1 to 0.5
- enter_a: bfloat16 [1536, 2048], P('expert'), may hold values from -6 to 6
- enter_grad: bfloat16 [1536, 2048], P('expert'), may hold values from -6 to 6
- w_gate: bfloat16 [4, 64, 2048, 768], P('segment', 'expert'), may hold values from -0.125 to 0.125
- w_up: bfloat16 [4, 64, 2048, 768], P('segment', 'expert'), may hold values from -0.125 to 0.125
- w_down: bfloat16 [4, 64, 768, 2048], P('segment', 'expert'), may hold values from -0.21875 to 0.21875
Outputs:
- fwd_one: bfloat16 [4, 1536, 2048], P('segment', 'expert')
- grad_one: bfloat16 [4, 1536, 2048], P('segment', 'expert')
- fwd_two: bfloat16 [4, 1536, 2048], P('segment', 'expert')
- grad_two: bfloat16 [4, 1536, 2048], P('segment', 'expert')
The draws below stay inside these ranges and needn't reach their ends.
Inputs may be any that keep to these rules, and one draw needn't show every extreme that they name: `route_a1`: in each row the 8 experts differ; in the 24 rows of one device of one section no expert is named more than 4 times, a bound that some block reaches. `route_b1`: as for route_a1. `route_a2`: as for route_a1. `route_b2`: as for route_a1.
All inputs are finite; a program needn't handle non-finite values.
Results may differ from the reference program's by a relative error of at most 0.0085.
Values may be sent and summed in bfloat16 or wider, within the bound.
No kernel may reach another device: no remote copies, remote signals or barrier semaphores. Data moves between devices by JAX's collectives and lax.ppermute only.
A program may use at most 128 MiB of HBM per device.

```python
import math
import jax
import jax.numpy as jnp
import numpy as np
from jax import lax

D = 2048
FF = 768
TOP = 8
TOK_DEV = 24
EXPERTS = 64
SEGMENTS = 4
CAP = 4
TOKENS = 1536
N_EXPERT = 64


def block_scale(rng, extent, cuts, smallest, top_value):
    def one(dim, parts):
        steps = jax.random.uniform(jax.random.fold_in(jax.random.fold_in(rng, 6), dim), (parts,), jnp.float32, smallest / len(cuts), top_value / len(cuts))
        return jnp.repeat(jnp.exp(steps), extent[dim] // parts).reshape((-1,) + (1,) * (len(extent) - dim - 1))

    gain = one(*cuts[0])
    for cut in cuts[1:]:
        gain = gain * one(*cut)
    return gain


def assign_block(rng, own, number, rows, amount, top, reach, slope):
    ranking = jax.random.permutation(rng, amount)
    crowded, usual = portions_of(amount, rows * top, reach, slope, True), portions_of(amount, rows * top, reach, slope, False)
    places = jnp.arange(amount)

    def named(sizes, offset_by):
        used = int((sizes > 0).sum())
        fixed = max(1, used // 4)
        shifted = fixed + (places - fixed + offset_by * (used - fixed)) % max(1, amount - fixed)
        return jnp.zeros((amount,), jnp.int32).at[ranking[jnp.where(places < fixed, places, shifted)]].set(jnp.asarray(sizes, jnp.int32))

    sizes = jnp.where(number % 4 == 0, named(crowded, number // 4), named(usual, number - number // 4 - 1))
    mixed = jax.random.permutation(jax.random.fold_in(own, 3), amount)
    source_of, sink = mixed[0:amount // 2 * 2:2], mixed[1:amount // 2 * 2:2]
    slack = jnp.minimum(sizes[source_of] - 1, reach - sizes[sink]) // 2
    slack = jnp.where((source_of == ranking[0]) | (sink == ranking[0]) | (sizes[sink] == 0), 0, jnp.maximum(slack, 0))
    shifted = jax.random.randint(jax.random.fold_in(own, 4), (amount // 2,), 0, 1 << 20) % (slack + 1)
    sizes = sizes.at[source_of].add(-shifted).at[sink].add(shifted)
    items = jnp.searchsorted(jnp.cumsum(sizes), jnp.arange(rows * top), side="right").astype(jnp.int32)
    table = items.reshape(top, rows).T
    table = table[jax.random.permutation(jax.random.fold_in(own, 1), rows)]
    offset_by = jax.random.randint(jax.random.fold_in(own, 2), (rows, 1), 0, top)
    return jnp.take_along_axis(table, (jnp.arange(top)[None, :] + offset_by) % top, axis=1)


def portions_of(amount, total, bound, skew, full):
    loads = [(1 << 20) // math.isqrt(grade ** skew) + 1 for grade in range(1, amount + 1)]
    largest = bound if full else min(bound, max(-(-total // amount), total * loads[0] // sum(loads)))
    least = 1 if total - largest >= amount - 1 else 0
    counts, spare = [largest] + [least] * (amount - 1), total - largest - least * (amount - 1)
    while spare > 0:
        movable = [i for i in range(1, amount) if counts[i] < largest] or [i for i in range(1, amount) if counts[i] < bound]
        whole, left = sum([loads[i] for i in movable]), spare
        for i in movable:
            extra = min(bound - counts[i], max(1, left * loads[i] // whole), spare)
            counts[i] = counts[i] + extra
            spare = spare - extra
    return np.array(counts)


def gaussian(stream_key, extent, deviation, bound, split=(), held_as=jnp.bfloat16):
    level = block_scale(stream_key, extent, split, -0.22, 0.18) if split else 1.0
    drawn = jax.random.normal(stream_key, extent, jnp.float32) * deviation * level
    return jnp.minimum(jnp.maximum(drawn, -bound), bound).astype(held_as)


def setup_inputs(seed: int = 0) -> dict:
    splits = jax.random.split(jax.random.key(seed), 18)
    act_a = gaussian(splits[0], (SEGMENTS, TOKENS, D), 1.0, 6.0, ((0, 4), (1, 64)))
    route_a1_keys = jax.random.split(jax.random.fold_in(splits[1], 1), SEGMENTS * TOKENS // TOK_DEV)
    route_a1_turns = jax.random.permutation(jax.random.fold_in(splits[1], 3), SEGMENTS * TOKENS // TOK_DEV)
    route_a1 = jax.vmap(lambda own, number: assign_block(jax.random.fold_in(splits[1], 2), own, number, TOK_DEV, EXPERTS, TOP, CAP, 2))(route_a1_keys, route_a1_turns).reshape((SEGMENTS, TOKENS, TOP))
    gate_a1 = jnp.clip(0.1 + 0.4 * jax.random.uniform(splits[2], (SEGMENTS, TOKENS, TOP), jnp.float32) ** block_scale(splits[2], (SEGMENTS, TOKENS, TOP), ((0, 4), (1, 64)), -0.2, 0.2), 0.1, 0.5)
    act_b1 = gaussian(splits[3], (SEGMENTS, TOKENS, D), 1.0, 6.0, ((0, 4), (1, 64)))
    route_b1_keys = jax.random.split(jax.random.fold_in(splits[4], 1), SEGMENTS * TOKENS // TOK_DEV)
    route_b1_turns = jax.random.permutation(jax.random.fold_in(splits[4], 3), SEGMENTS * TOKENS // TOK_DEV)
    route_b1 = jax.vmap(lambda own, number: assign_block(jax.random.fold_in(splits[4], 2), own, number, TOK_DEV, EXPERTS, TOP, CAP, 2))(route_b1_keys, route_b1_turns).reshape((SEGMENTS, TOKENS, TOP))
    gate_b1 = jnp.clip(0.1 + 0.4 * jax.random.uniform(splits[5], (SEGMENTS, TOKENS, TOP), jnp.float32) ** block_scale(splits[5], (SEGMENTS, TOKENS, TOP), ((0, 4), (1, 64)), -0.2, 0.2), 0.1, 0.5)
    grad_b1 = gaussian(splits[6], (SEGMENTS, TOKENS, D), 1.0, 6.0, ((0, 4), (1, 64)))
    act_b2 = gaussian(splits[7], (SEGMENTS, TOKENS, D), 1.0, 6.0, ((0, 4), (1, 64)))
    route_a2_keys = jax.random.split(jax.random.fold_in(splits[8], 1), SEGMENTS * TOKENS // TOK_DEV)
    route_a2_turns = jax.random.permutation(jax.random.fold_in(splits[8], 3), SEGMENTS * TOKENS // TOK_DEV)
    route_a2 = jax.vmap(lambda own, number: assign_block(jax.random.fold_in(splits[8], 2), own, number, TOK_DEV, EXPERTS, TOP, CAP, 2))(route_a2_keys, route_a2_turns).reshape((SEGMENTS, TOKENS, TOP))
    gate_a2 = jnp.clip(0.1 + 0.4 * jax.random.uniform(splits[9], (SEGMENTS, TOKENS, TOP), jnp.float32) ** block_scale(splits[9], (SEGMENTS, TOKENS, TOP), ((0, 4), (1, 64)), -0.2, 0.2), 0.1, 0.5)
    route_b2_keys = jax.random.split(jax.random.fold_in(splits[10], 1), SEGMENTS * TOKENS // TOK_DEV)
    route_b2_turns = jax.random.permutation(jax.random.fold_in(splits[10], 3), SEGMENTS * TOKENS // TOK_DEV)
    route_b2 = jax.vmap(lambda own, number: assign_block(jax.random.fold_in(splits[10], 2), own, number, TOK_DEV, EXPERTS, TOP, CAP, 2))(route_b2_keys, route_b2_turns).reshape((SEGMENTS, TOKENS, TOP))
    gate_b2 = jnp.clip(0.1 + 0.4 * jax.random.uniform(splits[11], (SEGMENTS, TOKENS, TOP), jnp.float32) ** block_scale(splits[11], (SEGMENTS, TOKENS, TOP), ((0, 4), (1, 64)), -0.2, 0.2), 0.1, 0.5)
    enter_a = gaussian(splits[12], (TOKENS, D), 1.0, 6.0, ((0, 64),))
    enter_grad = gaussian(splits[13], (TOKENS, D), 1.0, 6.0, ((0, 64),))
    w_gate = gaussian(splits[14], (SEGMENTS, EXPERTS, D, FF), D ** -0.5, 0.125, ((0, 4), (1, 64)))
    w_up = gaussian(splits[15], (SEGMENTS, EXPERTS, D, FF), D ** -0.5, 0.125, ((0, 4), (1, 64)))
    w_down = gaussian(splits[16], (SEGMENTS, EXPERTS, FF, D), FF ** -0.5, 0.21875, ((0, 4), (1, 64)))
    return dict(act_a=act_a, route_a1=route_a1, gate_a1=gate_a1, act_b1=act_b1, route_b1=route_b1, gate_b1=gate_b1, grad_b1=grad_b1, act_b2=act_b2, route_a2=route_a2, gate_a2=gate_a2, route_b2=route_b2, gate_b2=gate_b2, enter_a=enter_a, enter_grad=enter_grad, w_gate=w_gate, w_up=w_up, w_down=w_down)


def expert_forward(inputs, gate_mat, up_mat, down_mat):
    gate_pre = jnp.dot(inputs, gate_mat, preferred_element_type=jnp.float32)
    up_pre = jnp.dot(inputs, up_mat, preferred_element_type=jnp.float32)
    hidden = (jax.nn.silu(gate_pre) * up_pre).astype(jnp.bfloat16)
    return jnp.dot(hidden, down_mat, preferred_element_type=jnp.float32).astype(jnp.bfloat16)


def expert_backward(inputs, cotangent, gate_mat, up_mat, down_mat):
    gate_pre = jnp.dot(inputs, gate_mat, preferred_element_type=jnp.float32)
    up_pre = jnp.dot(inputs, up_mat, preferred_element_type=jnp.float32)
    sigma = jax.nn.sigmoid(gate_pre)
    d_hidden = jnp.dot(cotangent, down_mat.T, preferred_element_type=jnp.float32)
    d_gate = (d_hidden * up_pre * sigma * (1.0 + gate_pre * (1.0 - sigma))).astype(jnp.bfloat16)
    d_upper = (d_hidden * gate_pre * sigma).astype(jnp.bfloat16)
    total = jnp.dot(d_gate, gate_mat.T, preferred_element_type=jnp.float32)
    total = total + jnp.dot(d_upper, up_mat.T, preferred_element_type=jnp.float32)
    return total.astype(jnp.bfloat16)


def global_slots(route):
    blocks = route.reshape(N_EXPERT, TOK_DEV * TOP)
    onehot = (blocks[:, :, None] == jnp.arange(EXPERTS, dtype=jnp.int32)[None, None, :]).astype(jnp.int32)
    before = jnp.cumsum(onehot, axis=1) - onehot
    position = jnp.sum(before * onehot, axis=2)
    source = jnp.arange(N_EXPERT, dtype=jnp.int32)[:, None]
    slots = blocks * (N_EXPERT * CAP) + source * CAP + position
    return slots.reshape(-1).astype(jnp.int32)


def dispatch(values, slots):
    buffer = jnp.zeros((EXPERTS * N_EXPERT * CAP, D), jnp.bfloat16)
    buffer = buffer.at[slots].set(jnp.repeat(values, TOP, axis=0))
    return buffer.reshape(EXPERTS, N_EXPERT * CAP, D)


def gather_back(results, slots, gates):
    picked = jnp.take(results.reshape(-1, D), slots, axis=0).astype(jnp.float32)
    picked = picked.reshape(TOKENS, TOP, D)
    return jnp.sum(picked * gates[:, :, None], axis=1).astype(jnp.bfloat16)


def layer_forward(values, route, gates, gate_all, up_all, down_all):
    slots = global_slots(route)
    buffer = dispatch(values, slots)
    results = lax.map(lambda item: expert_forward(item[0], item[1], item[2], item[3]), (buffer, gate_all, up_all, down_all))
    return gather_back(results, slots, gates)


def layer_backward(values, route, gates, cotangent, gate_all, up_all, down_all):
    slots = global_slots(route)
    buffer = dispatch(values, slots)
    cot_buffer = dispatch(cotangent, slots)
    results = lax.map(lambda item: expert_backward(item[0], item[1], item[2], item[3], item[4]), (buffer, cot_buffer, gate_all, up_all, down_all))
    return gather_back(results, slots, gates)


def reference(act_a, route_a1, gate_a1, act_b1, route_b1, gate_b1, grad_b1, act_b2, route_a2, gate_a2, route_b2, gate_b2, enter_a, enter_grad, w_gate, w_up, w_down):
    fwd_list = []
    grad_list = []
    for section in range(SEGMENTS):
        fwd_list.append(layer_forward(act_a[section], route_a1[section], gate_a1[section], w_gate[section], w_up[section], w_down[section]))
        grad_list.append(layer_backward(act_b1[section], route_b1[section], gate_b1[section], grad_b1[section], w_gate[section], w_up[section], w_down[section]))
    fwd_next = []
    grad_next = []
    for section in range(SEGMENTS):
        incoming = enter_a if section == 0 else fwd_list[section - 1]
        arriving = enter_grad if section == SEGMENTS - 1 else grad_list[section + 1]
        fwd_next.append(layer_forward(incoming, route_a2[section], gate_a2[section], w_gate[section], w_up[section], w_down[section]))
        grad_next.append(layer_backward(act_b2[section], route_b2[section], gate_b2[section], arriving, w_gate[section], w_up[section], w_down[section]))
    return (jnp.stack(fwd_list), jnp.stack(grad_list), jnp.stack(fwd_next), jnp.stack(grad_next))
```

```python
import functools

import jax
import jax.numpy as jnp
from jax import lax
from jax.experimental import pallas as pl
from jax.experimental.pallas import tpu as pltpu
from jax.sharding import Mesh, PartitionSpec as P

TOP = 8
ROWS = 24
PAD = 32
NZ = 4
PLANE = 16
CAP = 4
SLOTS = PLANE * NZ * CAP
COLS = NZ * PAD
META = 16
F32 = jnp.float32
BF16 = jnp.bfloat16


def dot(a, b):
    return jnp.dot(a, b, preferred_element_type=F32)


def iota(shape, dim):
    return lax.broadcasted_iota(jnp.int32, shape, dim)


def halves(value):
    high = value.astype(BF16)
    rest = value - high.astype(F32)
    middle = rest.astype(BF16)
    low = (rest - middle.astype(F32)).astype(BF16)
    return high, middle, low


def pack_kernel(act, ra1, rb1, ra2, rb2, ga1, gb1, ga2, gb2, out):
    place = ((iota((ROWS, COLS), 1) % PAD) == iota((ROWS, COLS), 0)).astype(BF16)
    out[0:ROWS, :] = act[...]
    arrays = [r[...].astype(F32).astype(BF16) for r in (ra1, rb1, ra2, rb2)]
    for g in (ga1, gb1, ga2, gb2):
        arrays.extend(halves(g[...]))
    for i, block in enumerate(arrays):
        out[ROWS:PAD, COLS * i : COLS * (i + 1)] = dot(block, place).astype(BF16)


def meta_of(pieces, i):
    lane = iota((TOP, COLS), 1)
    total = jnp.zeros((TOP, COLS), F32)
    for k in range(NZ):
        part = pieces[k][ROWS:PAD, COLS * i : COLS * (i + 1)].astype(F32)
        total = total + jnp.where(lane // PAD == k, part, 0.0)
    return total


def ranks_of(pieces, zpos, i):
    lane = iota((TOP, COLS), 1)
    route = jnp.where(lane % PAD < ROWS, meta_of(pieces, i) - (zpos * PLANE).astype(F32), -1.0)
    expert = iota((PLANE, COLS), 0).astype(F32)
    hits = [(route[j : j + 1, :] == expert).astype(F32) for j in range(TOP)]
    named = sum(hits[1:], hits[0])
    before = iota((COLS, COLS), 0)
    after = iota((COLS, COLS), 1)
    earlier = ((before // PAD == after // PAD) & (before < after)).astype(BF16)
    rank = dot(named.astype(BF16), earlier)
    return named * (rank + 1.0), hits


def select_of(rank):
    row = iota((SLOTS, COLS), 0)
    col = iota((SLOTS, COLS), 1)
    target = jnp.where((row // CAP) % NZ == col // PAD, row % CAP + 1, -1).astype(F32)
    copies = (iota((SLOTS, PLANE), 0) // (NZ * CAP) == iota((SLOTS, PLANE), 1)).astype(BF16)
    return (dot(copies, rank.astype(BF16)) == target).astype(BF16)


def stack(pieces, offset=0):
    return jnp.concatenate([p[offset : offset + PAD, :] for p in pieces], axis=0)


def first_kernel(zpos, p0, p1, p2, p3, out):
    pieces = (p0, p1, p2, p3)
    rank, _ = ranks_of(pieces, zpos[0], 0)
    out[...] = dot(select_of(rank), stack(pieces)).astype(BF16)


def plan_kernel(zpos, p0, p1, p2, p3, select, weight):
    pieces = (p0, p1, p2, p3)
    copies = (iota((PLANE, SLOTS), 1) // (NZ * CAP) == iota((PLANE, SLOTS), 0)).astype(BF16)
    row = iota((COLS, SLOTS), 1)
    col = iota((COLS, SLOTS), 0)
    target = jnp.where((row // CAP) % NZ == col // PAD, row % CAP + 1, -1).astype(F32)
    for i in range(4):
        rank, hits = ranks_of(pieces, zpos[0], i)
        if i > 0:
            select[i - 1] = select_of(rank)
        mask = dot(rank.T.astype(BF16), copies) == target
        for part in range(3):
            gate = meta_of(pieces, 4 + 3 * i + part)
            named = sum(hits[j] * gate[j : j + 1, :] for j in range(TOP))
            spread = dot(named.T.astype(BF16), copies)
            weight[i, part] = jnp.where(mask, spread, 0.0).astype(BF16)


def dispatch_kernel(offset, select, p0, p1, p2, p3, out):
    out[...] = dot(select[...], stack((p0, p1, p2, p3), offset)).astype(BF16)


def combine_kernel(weight, rows, own, b1, b2, b3):
    values = rows[...]
    total = dot(weight[0], values) + dot(weight[1], values) + dot(weight[2], values)
    own[...] = total[0:ROWS]
    for k, out in ((1, b1), (2, b2), (3, b3)):
        out[...] = total[PAD * k : PAD * k + ROWS].astype(BF16)


def call(kernel, outs, scalars, *args):
    specs = [pl.BlockSpec(memory_space=pltpu.SMEM)] * len(scalars)
    specs += [pl.BlockSpec(memory_space=pltpu.VMEM)] * len(args)
    single = not isinstance(outs, (list, tuple))
    out_specs = pl.BlockSpec(memory_space=pltpu.VMEM)
    if not single:
        out_specs = [out_specs] * len(outs)
    return pl.pallas_call(
        kernel,
        out_shape=outs,
        in_specs=specs,
        out_specs=out_specs,
        compiler_params=pltpu.CompilerParams(vmem_limit_bytes=24 << 20),
    )(*scalars, *args)


def shaped(*shape, dtype=BF16):
    return jax.ShapeDtypeStruct(shape, dtype)


def expert_forward(inputs, gate_mat, up_mat, down_mat):
    gate_pre = dot(inputs, gate_mat)
    up_pre = dot(inputs, up_mat)
    hidden = (jax.nn.silu(gate_pre) * up_pre).astype(BF16)
    return dot(hidden, down_mat).astype(BF16)


def expert_backward(inputs, cotangent, gate_mat, up_mat, down_mat):
    gate_pre = dot(inputs, gate_mat)
    up_pre = dot(inputs, up_mat)
    sigma = jax.nn.sigmoid(gate_pre)
    d_hidden = dot(cotangent, down_mat.T)
    d_gate = (d_hidden * up_pre * sigma * (1.0 + gate_pre * (1.0 - sigma))).astype(BF16)
    d_upper = (d_hidden * gate_pre * sigma).astype(BF16)
    return (dot(d_gate, gate_mat.T) + dot(d_upper, up_mat.T)).astype(BF16)


def along_z(block, k):
    return lax.ppermute(block, "z", [(i, (i + k) % NZ) for i in range(NZ)])


def to_section(block, step, k):
    sections = lax.axis_size("segment")
    route = [
        (s * NZ + i, ((s + step) % sections) * NZ + (i + k) % NZ)
        for s in range(sections)
        for i in range(NZ)
    ]
    return lax.ppermute(block, ("segment", "z"), route)


def gather_z(block):
    return (block,) + tuple(along_z(block, k) for k in (1, 2, 3))


def plane(rows):
    block = rows.reshape(PLANE, NZ * CAP, rows.shape[-1])
    return lax.all_to_all(block, ("x", "y"), split_axis=0, concat_axis=0, tiled=True).reshape(
        rows.shape
    )


def after(value, *others):
    return lax.optimization_barrier((value,) + others)[0]


def shards(
    act_a,
    route_a1,
    gate_a1,
    act_b1,
    route_b1,
    gate_b1,
    grad_b1,
    act_b2,
    route_a2,
    gate_a2,
    route_b2,
    gate_b2,
    enter_a,
    enter_grad,
    w_gate,
    w_up,
    w_down,
):
    width = act_a.shape[2]
    mats = (w_gate[0, 0], w_up[0, 0], w_down[0, 0])
    zpos = lax.axis_index("z").astype(jnp.int32)[None]
    section = lax.axis_index("segment")
    last = lax.axis_size("segment") - 1
    buffer = shaped(SLOTS, width)

    def flip(value):
        return value[0].T

    pack = call(
        pack_kernel,
        shaped(PAD, width),
        (),
        act_a[0],
        *[flip(v) for v in (route_a1, route_b1, route_a2, route_b2)],
        *[flip(v) for v in (gate_a1, gate_b1, gate_a2, gate_b2)],
    )
    head = gather_z(pack)
    send_f1 = call(first_kernel, buffer, (zpos,), *head)
    blank = jnp.zeros((PAD - ROWS, width), BF16)
    rest = jnp.concatenate([act_b1[0], blank, grad_b1[0], blank, act_b2[0], blank], axis=0)
    rest = gather_z(rest)
    select, weight = call(
        plan_kernel,
        [shaped(3, SLOTS, COLS), shaped(4, 3, COLS, SLOTS)],
        (zpos,),
        *head,
    )

    def dispatch(i, pieces, offset=0):
        return call(
            functools.partial(dispatch_kernel, offset), buffer, (), select[i - 1], *pieces
        )

    def combine(i, rows):
        parts = call(
            combine_kernel,
            [shaped(ROWS, width, dtype=F32)] + [shaped(ROWS, width)] * 3,
            (),
            weight[i],
            rows,
        )
        back = [along_z(parts[k], -k) for k in (1, 2, 3)]
        total = parts[0] + back[0].astype(F32) + back[1].astype(F32) + back[2].astype(F32)
        return total.astype(BF16)

    def onward(value, step):
        value = jnp.concatenate([value, blank], axis=0)
        return tuple(to_section(value, step, k) for k in range(NZ))

    got_f1 = plane(send_f1)
    got_x1 = plane(after(dispatch(1, rest, 0), got_f1))
    out_f1 = expert_forward(got_f1, *mats)
    got_c1 = plane(after(dispatch(1, rest, PAD), got_x1))
    back_f1 = plane(after(out_f1, got_c1))
    out_b1 = expert_backward(got_x1, got_c1, *mats)
    back_b1 = plane(after(out_b1, back_f1))
    fwd_one = combine(0, back_f1)
    in_two = onward(jnp.where(section == last, enter_a, fwd_one), 1)
    got_x2 = plane(after(dispatch(3, rest, 2 * PAD), back_b1))
    grad_one = combine(1, back_b1)
    cot_two = onward(jnp.where(section == 0, enter_grad, grad_one), -1)
    got_f2 = plane(after(dispatch(2, in_two), got_x2))
    out_f2 = expert_forward(got_f2, *mats)
    got_c2 = plane(after(dispatch(3, cot_two), got_f2))
    back_f2 = plane(after(out_f2, got_c2))
    out_b2 = expert_backward(got_x2, got_c2, *mats)
    back_b2 = plane(after(out_b2, back_f2))
    fwd_two = combine(2, back_f2)
    grad_two = combine(3, back_b2)
    return fwd_one[None], grad_one[None], fwd_two[None], grad_two[None]


def solution(mesh):
    segments, experts = mesh.devices.shape
    side = int(round((experts // NZ) ** 0.5))
    grid = Mesh(
        mesh.devices.reshape(segments, NZ, side, experts // NZ // side),
        ("segment", "z", "x", "y"),
    )
    spread = ("z", "x", "y")
    tokens = P("segment", spread, None)
    weights = P("segment", spread, None, None)
    in_specs = (tokens,) * 12 + (P(spread, None),) * 2 + (weights,) * 3
    return jax.shard_map(
        shards, mesh=grid, in_specs=in_specs, out_specs=(tokens,) * 4, check_vma=False
    )
```

```python
import functools

import jax
import jax.numpy as jnp
from jax import lax
from jax.experimental import pallas as pl
from jax.experimental.pallas import tpu as pltpu
from jax.sharding import Mesh, PartitionSpec as P

TOP = 8
ROWS = 24
NZ = 4
SIDE = 4
PLANE = 16
CAP = 4
SLOTS = PLANE * NZ * CAP
TOKENS = NZ * ROWS
LANES = 128
PIECES = 4
F32 = jnp.float32
BF16 = jnp.bfloat16


def dot(a, b):
    return jnp.dot(a, b, preferred_element_type=F32)


def dot_t(a, b):
    return lax.dot_general(a, b, (((1,), (1,)), ((), ())), preferred_element_type=F32)


def iota(shape, dim):
    return lax.broadcasted_iota(jnp.int32, shape, dim)


def block_of(token):
    return sum((token >= ROWS * k).astype(jnp.int32) for k in range(1, NZ + 1))


def thirds(value):
    high = value.astype(BF16).astype(F32)
    rest = value - high
    middle = rest.astype(BF16).astype(F32)
    return high, middle, rest - middle


def pack_kernel(act, ra1, rb1, ra2, rb2, ga1, gb1, ga2, gb2, out, meta):
    width = act.shape[1]
    out[:, 0:width] = act[...]
    meta[...] = jnp.zeros_like(meta)
    arrays = [r[...].astype(F32) for r in (ra1, rb1, ra2, rb2)]
    for g in (ga1, gb1, ga2, gb2):
        arrays.extend(thirds(g[...]))
    for i, block in enumerate(arrays):
        meta[TOP * i : TOP * (i + 1), 0:ROWS] = block
    out[:, width : width + LANES] = meta[...].T[0:ROWS].astype(BF16)


def meta_of(pieces):
    parts = [p[...].astype(F32) for p in pieces]
    parts.append(jnp.zeros((LANES - TOKENS, LANES), F32))
    return jnp.concatenate(parts, axis=0).T


def ranks_of(meta, place, i):
    lane = iota((TOP, LANES), 1)
    zpos = place // PLANE
    route = meta[TOP * i : TOP * (i + 1)] - (zpos * PLANE).astype(F32)
    route = jnp.where(lane < TOKENS, route, -1.0)
    expert = iota((PLANE, LANES), 0).astype(F32)
    hits = [(route[j : j + 1, :] == expert).astype(F32) for j in range(TOP)]
    named = sum(hits[1:], hits[0])
    before = iota((LANES, LANES), 0)
    later = iota((LANES, LANES), 1)
    earlier = (block_of(before) == block_of(later)) & (before < later)
    rank = dot(named.astype(BF16), earlier.astype(F32).astype(BF16))
    return named * (rank + 1.0), hits


def select_of(rank):
    row = iota((SLOTS, LANES), 0)
    col = iota((SLOTS, LANES), 1)
    target = jnp.where((row // CAP) % NZ == block_of(col), row % CAP + 1, -1).astype(F32)
    copies = iota((SLOTS, PLANE), 0) // (NZ * CAP) == iota((SLOTS, PLANE), 1)
    spread = dot(copies.astype(F32).astype(BF16), rank.astype(BF16))
    return (spread == target).astype(F32).astype(BF16)


def stack(pieces):
    parts = [p[...].astype(F32) for p in pieces]
    parts.append(jnp.zeros((LANES - TOKENS, parts[0].shape[1]), F32))
    return jnp.concatenate(parts, axis=0).astype(BF16)


def first_kernel(place, m0, m1, m2, m3, p0, p1, p2, p3, out, select):
    @pl.when(pl.program_id(0) == 0)
    def _():
        rank, _ = ranks_of(meta_of((m0, m1, m2, m3)), place[0], 0)
        select[...] = select_of(rank)

    out[...] = dot(select[...], stack((p0, p1, p2, p3))).astype(BF16)


def plan_kernel(place, m0, m1, m2, m3, select, weight):
    meta = meta_of((m0, m1, m2, m3))
    copies = iota((PLANE, SLOTS), 1) // (NZ * CAP) == iota((PLANE, SLOTS), 0)
    copies = copies.astype(F32).astype(BF16)
    row = iota((LANES, SLOTS), 1)
    col = iota((LANES, SLOTS), 0)
    target = jnp.where((row // CAP) % NZ == block_of(col), row % CAP + 1, -1).astype(F32)
    for i in range(4):
        rank, hits = ranks_of(meta, place[0], i)
        if i > 0:
            select[i - 1] = select_of(rank)
        mask = dot(rank.T.astype(BF16), copies) == target
        for part in range(3):
            first = TOP * (4 + 3 * i + part)
            gate = meta[first : first + TOP]
            named = sum(hits[j] * gate[j : j + 1, :] for j in range(TOP))
            spread = dot(named.T.astype(BF16), copies)
            weight[i, part] = jnp.where(mask, spread, 0.0).astype(BF16)


def dispatch_kernel(select, p0, p1, p2, p3, out):
    out[...] = dot(select[0], stack((p0, p1, p2, p3))).astype(BF16)


def combine_kernel(weight, rows, own, b1, b2, b3):
    values = rows[...]
    total = sum(dot(weight[0, part], values) for part in range(3))
    own[...] = total[0:ROWS]
    for k, out in ((1, b1), (2, b2), (3, b3)):
        out[...] = total[ROWS * k : ROWS * (k + 1)].astype(BF16)


def sum_of(own, b1, b2, b3):
    total = own[...] + b1[...].astype(F32) + b2[...].astype(F32) + b3[...].astype(F32)
    return total.astype(BF16)


def sum_kernel(own, b1, b2, b3, out):
    out[...] = sum_of(own, b1, b2, b3)


def pass_kernel(edge, own, b1, b2, b3, enter, out, onward):
    total = sum_of(own, b1, b2, b3)
    out[...] = total
    onward[...] = total

    @pl.when(edge[0] == 1)
    def _():
        onward[...] = enter[...]


def pair_kernel(a, b, out):
    width = a.shape[1]
    out[:, 0:width] = a[...]
    out[:, width : 2 * width] = b[...]


def fetches(pairs, sems):
    groups = []
    for source, target in pairs:
        size = source.shape[0] // PIECES
        group = []
        for k in range(PIECES):
            part = pl.ds(size * k, size)
            sem = sems.at[PIECES * len(groups) + k]
            group.append(pltpu.make_async_copy(source.at[part], target.at[part], sem))
        groups.append(group)
    for group in groups:
        for copy in group:
            copy.start()
    return groups


def arrive(*groups):
    for group in groups:
        for copy in group:
            copy.wait()


def forward_kernel(rows, w_gate, w_up, w_down, result, *scratch):
    x, gate_mat, up_mat, down_mat, out, sems, sent = scratch
    mats = ((w_gate, gate_mat), (w_up, up_mat), (w_down, down_mat))
    inputs, gates, ups, downs = fetches(((rows, x),) + mats, sems)
    arrive(inputs, gates)
    gate_pre = dot(x[...], gate_mat[...])
    arrive(ups)
    hidden = (jax.nn.silu(gate_pre) * dot(x[...], up_mat[...])).astype(BF16)
    arrive(downs)
    size = out.shape[1] // PIECES
    sends = []
    for j in range(PIECES):
        cols = pl.ds(size * j, size)
        out[:, cols] = dot(hidden, down_mat[:, cols]).astype(BF16)
        copy = pltpu.make_async_copy(out.at[:, cols], result.at[:, cols], sent.at[j])
        copy.start()
        sends.append(copy)
    arrive(sends)


def backward_kernel(column, xs, cs, w_gate, w_up, w_down, result, *scratch):
    x, c, gate_mat, up_mat, down_mat, out, sems, sent = scratch
    width = x.shape[1]
    inputs = ((xs.at[:, pl.ds(0, width)], x), (cs.at[:, pl.ds(column * width, width)], c))
    mats = ((w_gate, gate_mat), (w_up, up_mat), (w_down, down_mat))
    rows, gates, ups, cots, downs = fetches(
        (inputs[0], mats[0], mats[1], inputs[1], mats[2]), sems
    )
    arrive(rows, gates)
    gate_pre = dot(x[...], gate_mat[...])
    arrive(ups)
    up_pre = dot(x[...], up_mat[...])
    arrive(cots, downs)
    sigma = jax.nn.sigmoid(gate_pre)
    d_hidden = dot_t(c[...], down_mat[...])
    d_gate = (d_hidden * up_pre * sigma * (1.0 + gate_pre * (1.0 - sigma))).astype(BF16)
    d_upper = (d_hidden * gate_pre * sigma).astype(BF16)
    size = width // PIECES
    sends = []
    for j in range(PIECES):
        cols = pl.ds(size * j, size)
        part = dot_t(d_gate, gate_mat[cols, :]) + dot_t(d_upper, up_mat[cols, :])
        out[:, cols] = part.astype(BF16)
        copy = pltpu.make_async_copy(out.at[:, cols], result.at[:, cols], sent.at[j])
        copy.start()
        sends.append(copy)
    arrive(sends)


SMEM = pl.BlockSpec(memory_space=pltpu.SMEM)
ANY = pl.BlockSpec(memory_space=pl.ANY)
HBM = pl.BlockSpec(memory_space=pltpu.HBM)


def spec(shape, index):
    return pl.BlockSpec(shape, index)


def whole(array):
    zeros = (0,) * len(array.shape)
    return pl.BlockSpec(tuple(array.shape), lambda *_: zeros)


def shaped(*shape, dtype=BF16):
    return jax.ShapeDtypeStruct(shape, dtype)


def after(value, *others):
    return lax.optimization_barrier((value,) + others)[0]


def call(
    line, kernel, name, grid, in_specs, args, out_specs, outs, scratch=(), flops=0, room=16
):
    if line:
        args = (after(args[0], line[-1]),) + tuple(args[1:])
    moved = sum(a.size * a.dtype.itemsize for a in args)
    moved += sum(o.size * o.dtype.itemsize for o in outs)
    results = pl.pallas_call(
        kernel,
        name=name,
        grid=grid,
        in_specs=in_specs,
        out_specs=out_specs,
        out_shape=outs,
        scratch_shapes=scratch,
        cost_estimate=pl.CostEstimate(flops=flops, bytes_accessed=moved, transcendentals=0),
        compiler_params=pltpu.CompilerParams(
            vmem_limit_bytes=room << 20, dimension_semantics=("arbitrary",) * len(grid)
        ),
    )(*args)
    line.append(results[0])
    return results


def shift(block, axis, k):
    size = lax.axis_size(axis)
    return lax.ppermute(block, axis, [(i, (i + k) % size) for i in range(size)])


def to_section(block, step, k):
    sections = lax.axis_size("segment")
    route = [
        (s * NZ + i, ((s + step) % sections) * NZ + (i + k) % NZ)
        for s in range(sections)
        for i in range(NZ)
    ]
    return lax.ppermute(block, ("segment", "z"), route)


def gather_z(block):
    return (block,) + tuple(shift(block, "z", k) for k in (1, 2, 3))


def plane(rows):
    block = rows.reshape(PLANE, NZ * CAP, rows.shape[-1])
    return lax.all_to_all(block, ("x", "y"), split_axis=0, concat_axis=0, tiled=True).reshape(
        rows.shape
    )


def shards(
    act_a,
    route_a1,
    gate_a1,
    act_b1,
    route_b1,
    gate_b1,
    grad_b1,
    act_b2,
    route_a2,
    gate_a2,
    route_b2,
    gate_b2,
    enter_a,
    enter_grad,
    w_gate,
    w_up,
    w_down,
):
    width = act_a.shape[2]
    hidden = w_gate.shape[3]
    mats = (w_gate[0, 0], w_up[0, 0], w_down[0, 0])
    place = lax.axis_index(("z", "x", "y")).astype(jnp.int32)[None]
    section = lax.axis_index("segment")
    last = lax.axis_size("segment") - 1
    half = width // 2
    buffer = shaped(SLOTS, width)
    slot_specs = [spec((SLOTS, half), lambda i: (0, i))]
    row_specs = [spec((ROWS, half), lambda i: (0, i))] * NZ

    line = []
    run = functools.partial(call, line)
    args = (act_a[0],) + tuple(
        v[0].T
        for v in (route_a1, route_b1, route_a2, route_b2, gate_a1, gate_b1, gate_a2, gate_b2)
    )
    packed = shaped(ROWS, width + LANES)
    (head,) = run(
        pack_kernel,
        "pack",
        (1,),
        [whole(a) for a in args],
        args,
        [whole(packed)],
        [packed],
        [pltpu.VMEM((LANES, LANES), F32)],
        room=60,
    )
    head = gather_z(head)
    pair = shaped(ROWS, 2 * width)
    (both,) = run(
        pair_kernel,
        "pair",
        (1,),
        [whole(act_b1[0])] * 2,
        (act_b1[0], grad_b1[0]),
        [whole(pair)],
        [pair],
    )
    meta_specs = [spec((ROWS, LANES), lambda i: (0, width // LANES))] * NZ
    (send_f1,) = run(
        first_kernel,
        "first",
        (2,),
        [SMEM] + meta_specs + row_specs,
        (place,) + head + head,
        slot_specs,
        [buffer],
        [pltpu.VMEM((SLOTS, LANES), BF16)],
    )
    both = gather_z(after(both, *head))
    plans = [shaped(3, SLOTS, LANES), shaped(4, 3, LANES, SLOTS)]
    select, weight = run(
        plan_kernel,
        "plan",
        (1,),
        [SMEM] + meta_specs,
        (place,) + head,
        [whole(p) for p in plans],
        plans,
    )

    def dispatch(i, pieces):
        size = pieces[0].shape[1]
        (rows,) = run(
            dispatch_kernel,
            "dispatch",
            (size // half,),
            [spec((1, SLOTS, LANES), lambda _: (i - 1, 0, 0))]
            + [spec((ROWS, half), lambda j: (0, j))] * NZ,
            (select,) + tuple(pieces),
            slot_specs,
            [shaped(SLOTS, size)],
        )
        return rows

    def combine(i, rows):
        parts = run(
            combine_kernel,
            "combine",
            (2,),
            [spec((1, 3, LANES, SLOTS), lambda _: (i, 0, 0, 0))] + slot_specs,
            (weight, rows),
            row_specs,
            [shaped(ROWS, width, dtype=F32)] + [shaped(ROWS, width)] * 3,
        )
        return [parts[0]] + [shift(parts[k], "z", -k) for k in (1, 2, 3)]

    def finish(parts):
        out = shaped(ROWS, width)
        (total,) = run(
            sum_kernel, "sum", (1,), [whole(p) for p in parts], parts, [whole(out)], [out]
        )
        return total

    def onward(parts, edge, enter, step):
        out = shaped(ROWS, width)
        args = (edge.astype(jnp.int32)[None],) + tuple(parts) + (enter,)
        total, moving = run(
            pass_kernel,
            "pass",
            (1,),
            [SMEM] + [whole(a) for a in args[1:]],
            args,
            [whole(out)] * 2,
            [out] * 2,
        )
        return total, [to_section(moving, step, k) for k in range(NZ)]

    rows_buffer = pltpu.VMEM((SLOTS, width), BF16)
    mat_buffers = [pltpu.VMEM(m.shape, BF16) for m in mats]

    def forward(rows):
        (out,) = run(
            forward_kernel,
            "forward",
            (),
            [ANY] + [HBM] * 3,
            (rows,) + mats,
            [ANY],
            [buffer],
            [rows_buffer]
            + mat_buffers
            + [
                rows_buffer,
                pltpu.SemaphoreType.DMA((4 * PIECES,)),
                pltpu.SemaphoreType.DMA((PIECES,)),
            ],
            6 * SLOTS * width * hidden,
            room=60,
        )
        return out

    def backward(x, c, column):
        (out,) = run(
            functools.partial(backward_kernel, column),
            "backward",
            (),
            [ANY] * 2 + [HBM] * 3,
            (x, c) + mats,
            [ANY],
            [shaped(SLOTS, width)],
            [rows_buffer, rows_buffer]
            + mat_buffers
            + [
                rows_buffer,
                pltpu.SemaphoreType.DMA((5 * PIECES,)),
                pltpu.SemaphoreType.DMA((PIECES,)),
            ],
            10 * SLOTS * width * hidden,
            room=60,
        )
        return out

    at_f1 = plane(send_f1)
    at_b1 = plane(after(dispatch(1, both), at_f1))
    out_f1 = forward(at_f1)
    x_two = gather_z(after(act_b2[0], out_f1))
    back_f1 = plane(after(out_f1, at_b1))
    send_x2 = dispatch(3, x_two)
    back_b1 = plane(after(backward(at_b1, at_b1, 1), back_f1))
    parts_f = combine(0, back_f1)
    at_x2 = plane(after(send_x2, back_b1, parts_f[0]))
    parts_b = combine(1, back_b1)
    fwd_one, in_two = onward(parts_f, section == last, enter_a, 1)
    grad_one, cot_two = onward(parts_b, section == 0, enter_grad, -1)
    at_f2 = plane(after(dispatch(2, in_two), at_x2))
    at_c2 = plane(after(dispatch(3, cot_two), at_f2))
    back_f2 = plane(after(forward(at_f2), at_c2))
    back_b2 = plane(after(backward(at_x2, at_c2, 0), back_f2))
    fwd_two = finish(combine(2, back_f2))
    grad_two = finish(combine(3, back_b2))
    return fwd_one[None], grad_one[None], fwd_two[None], grad_two[None]


def solution(mesh):
    segments, experts = mesh.devices.shape
    grid = Mesh(
        mesh.devices.reshape(segments, NZ, SIDE, experts // NZ // SIDE),
        ("segment", "z", "x", "y"),
    )
    spread = ("z", "x", "y")
    tokens = P("segment", spread, None)
    weights = P("segment", spread, None, None)
    in_specs = (tokens,) * 12 + (P(spread, None),) * 2 + (weights,) * 3
    return jax.shard_map(
        shards, mesh=grid, in_specs=in_specs, out_specs=(tokens,) * 4, check_vma=False
    )
```

```python
import functools

import jax
import jax.numpy as jnp
from jax import lax
from jax.experimental import pallas as pl
from jax.experimental.pallas import tpu as pltpu
from jax.sharding import Mesh, PartitionSpec as P

TOP = 8
ROWS = 24
NZ = 4
SIDE = 4
PLANE = 16
CAP = 4
SLOTS = PLANE * NZ * CAP
TOKENS = NZ * ROWS
LANES = 128
PIECES = 4
THIRDS = 3
F32 = jnp.float32
BF16 = jnp.bfloat16


def dot(a, b):
    return jnp.dot(a, b, preferred_element_type=F32)


def dot_t(a, b):
    return lax.dot_general(a, b, (((1,), (1,)), ((), ())), preferred_element_type=F32)


def iota(shape, dim):
    return lax.broadcasted_iota(jnp.int32, shape, dim)


def block_of(token):
    return sum((token >= ROWS * k).astype(jnp.int32) for k in range(1, NZ + 1))


def thirds(value):
    high = value.astype(BF16).astype(F32)
    rest = value - high
    middle = rest.astype(BF16).astype(F32)
    return high, middle, rest - middle


def pack_kernel(act, grad, ra1, rb1, ra2, rb2, ga1, gb1, ga2, gb2, out, meta):
    width = act.shape[1]
    out[:, 0:width] = act[...]
    out[:, width : 2 * width] = grad[...]
    meta[...] = jnp.zeros_like(meta)
    arrays = [r[...].astype(F32) for r in (ra1, rb1, ra2, rb2)]
    for g in (ga1, gb1, ga2, gb2):
        arrays.extend(thirds(g[...]))
    for i, block in enumerate(arrays):
        meta[TOP * i : TOP * (i + 1), 0:ROWS] = block
    out[:, 2 * width : 2 * width + LANES] = meta[...].T[0:ROWS].astype(BF16)


def meta_of(pieces):
    parts = [p[...].astype(F32) for p in pieces]
    parts.append(jnp.zeros((LANES - TOKENS, LANES), F32))
    return jnp.concatenate(parts, axis=0).T


def ranks_of(meta, place, i):
    lane = iota((TOP, LANES), 1)
    zpos = place // PLANE
    route = meta[TOP * i : TOP * (i + 1)] - (zpos * PLANE).astype(F32)
    route = jnp.where(lane < TOKENS, route, -1.0)
    expert = iota((PLANE, LANES), 0).astype(F32)
    hits = [(route[j : j + 1, :] == expert).astype(F32) for j in range(TOP)]
    named = sum(hits[1:], hits[0])
    before = iota((LANES, LANES), 0)
    later = iota((LANES, LANES), 1)
    earlier = (block_of(before) == block_of(later)) & (before < later)
    rank = dot(named.astype(BF16), earlier.astype(F32).astype(BF16))
    return named * (rank + 1.0), hits


def select_of(rank):
    row = iota((SLOTS, LANES), 0)
    col = iota((SLOTS, LANES), 1)
    target = jnp.where((row // CAP) % NZ == block_of(col), row % CAP + 1, -1).astype(F32)
    copies = iota((SLOTS, PLANE), 0) // (NZ * CAP) == iota((SLOTS, PLANE), 1)
    spread = dot(copies.astype(F32).astype(BF16), rank.astype(BF16))
    return (spread == target).astype(F32).astype(BF16)


def stack(pieces):
    parts = [p[...].astype(F32) for p in pieces]
    parts.append(jnp.zeros((LANES - TOKENS, parts[0].shape[1]), F32))
    return jnp.concatenate(parts, axis=0).astype(BF16)


def first_kernel(place, m0, m1, m2, m3, p0, p1, p2, p3, out, select):
    @pl.when(pl.program_id(0) == 0)
    def _():
        rank, _ = ranks_of(meta_of((m0, m1, m2, m3)), place[0], 1)
        select[...] = select_of(rank)

    out[...] = dot(select[...], stack((p0, p1, p2, p3))).astype(BF16)


def plan_kernel(place, m0, m1, m2, m3, select, weight):
    meta = meta_of((m0, m1, m2, m3))
    copies = iota((PLANE, SLOTS), 1) // (NZ * CAP) == iota((PLANE, SLOTS), 0)
    copies = copies.astype(F32).astype(BF16)
    row = iota((LANES, SLOTS), 1)
    col = iota((LANES, SLOTS), 0)
    target = jnp.where((row // CAP) % NZ == block_of(col), row % CAP + 1, -1).astype(F32)
    for i in range(4):
        rank, hits = ranks_of(meta, place[0], i)
        if i != 1:
            select[i - i // 2] = select_of(rank)
        mask = dot(rank.T.astype(BF16), copies) == target
        for part in range(3):
            first = TOP * (4 + 3 * i + part)
            gate = meta[first : first + TOP]
            named = sum(hits[j] * gate[j : j + 1, :] for j in range(TOP))
            spread = dot(named.T.astype(BF16), copies)
            weight[i, part] = jnp.where(mask, spread, 0.0).astype(BF16)


def dispatch_kernel(select, p0, p1, p2, p3, out):
    out[...] = dot(select[0], stack((p0, p1, p2, p3))).astype(BF16)


def combine_kernel(weight, rows, own, b1, b2, b3):
    values = rows[...]
    total = sum(dot(weight[0, part], values) for part in range(3))
    own[...] = total[0:ROWS]
    for k, out in ((1, b1), (2, b2), (3, b3)):
        out[...] = total[ROWS * k : ROWS * (k + 1)].astype(BF16)


def sum_of(own, b1, b2, b3):
    total = own[...] + b1[...].astype(F32) + b2[...].astype(F32) + b3[...].astype(F32)
    return total.astype(BF16)


def sum_kernel(own, b1, b2, b3, out):
    out[...] = sum_of(own, b1, b2, b3)


def pass_kernel(edge, own, b1, b2, b3, enter, out, onward):
    total = sum_of(own, b1, b2, b3)
    out[...] = total
    onward[...] = total

    @pl.when(edge[0] == 1)
    def _():
        onward[...] = enter[...]


def part(ref, k):
    size = ref.shape[0] // PIECES
    return ref.at[pl.ds(pl.multiple_of(size * k, size), size)]


def fetch(pair, sems, k):
    source, target = pair
    return pltpu.make_async_copy(part(source, k), part(target, k), sems.at[k])


def column(ref, k):
    size = ref.shape[1] // PIECES
    return ref.at[:, pl.ds(pl.multiple_of(size * k, size), size)]


def loop(body, count=PIECES):
    lax.fori_loop(0, count, lambda k, _: body(k), None)


def begin(whole, pieces, sems, semp):
    for i, (source, target) in enumerate(whole):
        pltpu.make_async_copy(source, target, sems.at[i]).start()
    for k in range(PIECES):
        for i, pair in enumerate(pieces):
            fetch(pair, semp.at[i], k).start()


def pre_activations(x, gate, up, semp, gate_pre, up_pre):
    gate_pre[...] = jnp.zeros_like(gate_pre)
    up_pre[...] = jnp.zeros_like(up_pre)

    def step(k):
        for i, (pair, total) in enumerate(((gate, gate_pre), (up, up_pre))):
            fetch(pair, semp.at[i], k).wait()
            total[...] += dot(column(x, k)[...], part(pair[1], k)[...])

    loop(step)


def send(out, result, sent, k):
    return pltpu.make_async_copy(column(out, k), column(result, k), sent.at[k])


def forward_kernel(rows, w_gate, w_up, w_down, result, *scratch):
    x, gate_mat, up_mat, down_mat, out, gate_pre, up_pre, hidden, sems, semp, sent = scratch
    whole = ((rows, x), (w_down, down_mat))
    gate, up = (w_gate, gate_mat), (w_up, up_mat)
    begin(whole[:1], (gate, up), sems, semp)
    pltpu.make_async_copy(w_down, down_mat, sems.at[1]).start()
    pltpu.make_async_copy(rows, x, sems.at[0]).wait()
    pre_activations(x, gate, up, semp, gate_pre, up_pre)
    hidden[...] = (jax.nn.silu(gate_pre[...]) * up_pre[...]).astype(BF16)
    pltpu.make_async_copy(w_down, down_mat, sems.at[1]).wait()

    def step(k):
        column(out, k)[...] = dot(hidden[...], column(down_mat, k)[...]).astype(BF16)
        send(out, result, sent, k).start()

    loop(step)
    for k in range(PIECES):
        send(out, result, sent, k).wait()


def backward_kernel(place, xs, cs, w_gate, w_up, w_down, result, *scratch):
    x, c, gate_mat, up_mat, down_mat, out = scratch[:6]
    gate_pre, up_pre, d_gate, d_upper, sems, semp, sent = scratch[6:]
    width = x.shape[1]
    gate, up = (w_gate, gate_mat), (w_up, up_mat)
    rows = pltpu.make_async_copy(xs.at[:, pl.ds(0, width)], x, sems.at[0])
    cots = pltpu.make_async_copy(cs.at[:, pl.ds(place * width, width)], c, sems.at[1])
    downs = pltpu.make_async_copy(w_down, down_mat, sems.at[2])
    rows.start()
    begin((), (gate, up), sems, semp)
    cots.start()
    downs.start()
    rows.wait()
    pre_activations(x, gate, up, semp, gate_pre, up_pre)
    cots.wait()
    downs.wait()
    size = down_mat.shape[0] // THIRDS

    def inner(k):
        cols = pl.ds(pl.multiple_of(size * k, size), size)
        d_hidden = dot_t(c[...], down_mat[cols, :])
        g, u = gate_pre[:, cols], up_pre[:, cols]
        sigma = jax.nn.sigmoid(g)
        d_gate[:, cols] = (d_hidden * u * sigma * (1.0 + g * (1.0 - sigma))).astype(BF16)
        d_upper[:, cols] = (d_hidden * g * sigma).astype(BF16)

    loop(inner, THIRDS)

    def step(k):
        total = dot_t(d_gate[...], part(gate_mat, k)[...])
        total = total + dot_t(d_upper[...], part(up_mat, k)[...])
        column(out, k)[...] = total.astype(BF16)
        send(out, result, sent, k).start()

    loop(step)
    for k in range(PIECES):
        send(out, result, sent, k).wait()


SMEM = pl.BlockSpec(memory_space=pltpu.SMEM)
ANY = pl.BlockSpec(memory_space=pl.ANY)
HBM = pl.BlockSpec(memory_space=pltpu.HBM)


def spec(shape, index):
    return pl.BlockSpec(shape, index)


def whole(array):
    zeros = (0,) * len(array.shape)
    return pl.BlockSpec(tuple(array.shape), lambda *_: zeros)


def shaped(*shape, dtype=BF16):
    return jax.ShapeDtypeStruct(shape, dtype)


def after(value, *others):
    return lax.optimization_barrier((value,) + others)[0]


def call(
    line, kernel, name, grid, in_specs, args, out_specs, outs, scratch=(), flops=0, room=16
):
    if line:
        args = (after(args[0], line[-1]),) + tuple(args[1:])
    moved = sum(a.size * a.dtype.itemsize for a in args)
    moved += sum(o.size * o.dtype.itemsize for o in outs)
    results = pl.pallas_call(
        kernel,
        name=name,
        grid=grid,
        in_specs=in_specs,
        out_specs=out_specs,
        out_shape=outs,
        scratch_shapes=scratch,
        cost_estimate=pl.CostEstimate(flops=flops, bytes_accessed=moved, transcendentals=0),
        compiler_params=pltpu.CompilerParams(
            vmem_limit_bytes=room << 20, dimension_semantics=("arbitrary",) * len(grid)
        ),
    )(*args)
    line.append(results[0])
    return results


def shift(block, axis, k):
    size = lax.axis_size(axis)
    return lax.ppermute(block, axis, [(i, (i + k) % size) for i in range(size)])


def to_section(block, step, k):
    sections = lax.axis_size("segment")
    route = [
        (s * NZ + i, ((s + step) % sections) * NZ + (i + k) % NZ)
        for s in range(sections)
        for i in range(NZ)
    ]
    return lax.ppermute(block, ("segment", "z"), route)


def gather_z(block):
    return (block,) + tuple(shift(block, "z", k) for k in (1, 2, 3))


def plane(rows):
    block = rows.reshape(PLANE, NZ * CAP, rows.shape[-1])
    return lax.all_to_all(block, ("x", "y"), split_axis=0, concat_axis=0, tiled=True).reshape(
        rows.shape
    )


def shards(
    act_a,
    route_a1,
    gate_a1,
    act_b1,
    route_b1,
    gate_b1,
    grad_b1,
    act_b2,
    route_a2,
    gate_a2,
    route_b2,
    gate_b2,
    enter_a,
    enter_grad,
    w_gate,
    w_up,
    w_down,
):
    width = act_a.shape[2]
    hidden = w_gate.shape[3]
    mats = (w_gate[0, 0], w_up[0, 0], w_down[0, 0])
    place = lax.axis_index(("z", "x", "y")).astype(jnp.int32)[None]
    section = lax.axis_index("segment")
    last = lax.axis_size("segment") - 1
    half = width // 2
    buffer = shaped(SLOTS, width)
    slot_specs = [spec((SLOTS, half), lambda i: (0, i))]
    row_specs = [spec((ROWS, half), lambda i: (0, i))] * NZ

    line = []
    run = functools.partial(call, line)
    args = (act_b1[0], grad_b1[0]) + tuple(
        v[0].T
        for v in (route_a1, route_b1, route_a2, route_b2, gate_a1, gate_b1, gate_a2, gate_b2)
    )
    packed = shaped(ROWS, 2 * width + LANES)
    (head,) = run(
        pack_kernel,
        "pack",
        (1,),
        [whole(a) for a in args],
        args,
        [whole(packed)],
        [packed],
        [pltpu.VMEM((LANES, LANES), F32)],
        room=60,
    )
    head = gather_z(head)
    meta_specs = [spec((ROWS, LANES), lambda i: (0, 2 * width // LANES))] * NZ
    (send_b1,) = run(
        first_kernel,
        "first",
        (4,),
        [SMEM] + meta_specs + row_specs,
        (place,) + head + head,
        slot_specs,
        [shaped(SLOTS, 2 * width)],
        [pltpu.VMEM((SLOTS, LANES), BF16)],
    )
    plans = [shaped(3, SLOTS, LANES), shaped(4, 3, LANES, SLOTS)]
    select, weight = run(
        plan_kernel,
        "plan",
        (1,),
        [SMEM] + meta_specs,
        (place,) + head,
        [whole(p) for p in plans],
        plans,
    )

    def dispatch(i, pieces):
        size = pieces[0].shape[1]
        (rows,) = run(
            dispatch_kernel,
            "dispatch",
            (size // half,),
            [spec((1, SLOTS, LANES), lambda _: (i - i // 2, 0, 0))]
            + [spec((ROWS, half), lambda j: (0, j))] * NZ,
            (select,) + tuple(pieces),
            slot_specs,
            [shaped(SLOTS, size)],
        )
        return rows

    def combine(i, rows):
        parts = run(
            combine_kernel,
            "combine",
            (2,),
            [spec((1, 3, LANES, SLOTS), lambda _: (i, 0, 0, 0))] + slot_specs,
            (weight, rows),
            row_specs,
            [shaped(ROWS, width, dtype=F32)] + [shaped(ROWS, width)] * 3,
        )
        return [parts[0]] + [shift(parts[k], "z", -k) for k in (1, 2, 3)]

    def finish(parts):
        out = shaped(ROWS, width)
        (total,) = run(
            sum_kernel, "sum", (1,), [whole(p) for p in parts], parts, [whole(out)], [out]
        )
        return total

    def onward(parts, edge, enter, step):
        out = shaped(ROWS, width)
        args = (edge.astype(jnp.int32)[None],) + tuple(parts) + (enter,)
        total, moving = run(
            pass_kernel,
            "pass",
            (1,),
            [SMEM] + [whole(a) for a in args[1:]],
            args,
            [whole(out)] * 2,
            [out] * 2,
        )
        return total, [to_section(moving, step, k) for k in range(NZ)]

    rows_buffer = pltpu.VMEM((SLOTS, width), BF16)
    wide_buffer = pltpu.VMEM((SLOTS, hidden), F32)
    thin_buffer = pltpu.VMEM((SLOTS, hidden), BF16)
    mat_buffers = [pltpu.VMEM(m.shape, BF16) for m in mats]

    def forward(rows):
        (out,) = run(
            forward_kernel,
            "forward",
            (),
            [ANY] + [HBM] * 3,
            (rows,) + mats,
            [ANY],
            [buffer],
            [rows_buffer]
            + mat_buffers
            + [
                rows_buffer,
                wide_buffer,
                wide_buffer,
                thin_buffer,
                pltpu.SemaphoreType.DMA((2,)),
                pltpu.SemaphoreType.DMA((2, PIECES)),
                pltpu.SemaphoreType.DMA((PIECES,)),
            ],
            6 * SLOTS * width * hidden,
            room=60,
        )
        return out

    def backward(x, c, column):
        (out,) = run(
            functools.partial(backward_kernel, column),
            "backward",
            (),
            [ANY] * 2 + [HBM] * 3,
            (x, c) + mats,
            [ANY],
            [shaped(SLOTS, width)],
            [rows_buffer, rows_buffer]
            + mat_buffers
            + [
                rows_buffer,
                wide_buffer,
                wide_buffer,
                thin_buffer,
                thin_buffer,
                pltpu.SemaphoreType.DMA((3,)),
                pltpu.SemaphoreType.DMA((2, PIECES)),
                pltpu.SemaphoreType.DMA((PIECES,)),
            ],
            10 * SLOTS * width * hidden,
            room=60,
        )
        return out

    at_b1 = plane(send_b1)
    a_one, x_two = gather_z(after(act_a[0], line[-1])), gather_z(after(act_b2[0], line[-1]))
    send_f1 = dispatch(0, a_one)
    send_x2 = dispatch(3, x_two)
    at_f1 = plane(after(send_f1, at_b1, send_x2))
    back_b1 = plane(after(backward(at_b1, at_b1, 1), at_f1))
    back_f1 = plane(after(forward(at_f1), back_b1))
    parts_b = combine(1, back_b1)
    grad_one, cot_two = onward(parts_b, section == 0, enter_grad, -1)
    at_x2 = plane(after(send_x2, back_f1, grad_one))
    parts_f = combine(0, back_f1)
    fwd_one, in_two = onward(parts_f, section == last, enter_a, 1)
    at_c2 = plane(after(dispatch(3, cot_two), at_x2))
    at_f2 = plane(after(dispatch(2, in_two), at_c2))
    back_b2 = plane(after(backward(at_x2, at_c2, 0), at_f2))
    back_f2 = plane(after(forward(at_f2), back_b2))
    grad_two = finish(combine(3, back_b2))
    fwd_two = finish(combine(2, back_f2))
    return fwd_one[None], grad_one[None], fwd_two[None], grad_two[None]


def solution(mesh):
    segments, experts = mesh.devices.shape
    grid = Mesh(
        mesh.devices.reshape(segments, NZ, SIDE, experts // NZ // SIDE),
        ("segment", "z", "x", "y"),
    )
    spread = ("z", "x", "y")
    tokens = P("segment", spread, None)
    weights = P("segment", spread, None, None)
    in_specs = (tokens,) * 12 + (P(spread, None),) * 2 + (weights,) * 3
    return jax.shard_map(
        shards, mesh=grid, in_specs=in_specs, out_specs=(tokens,) * 4, check_vma=False
    )
```

```python
import functools

import jax
import jax.numpy as jnp
from jax import lax
from jax.experimental import pallas as pl
from jax.experimental.pallas import tpu as pltpu
from jax.sharding import Mesh, PartitionSpec as P

TOP = 8
ROWS = 24
NZ = 4
SIDE = 4
PLANE = 16
CAP = 4
SLOTS = PLANE * NZ * CAP
TOKENS = NZ * ROWS
LANES = 128
PIECES = 4
THIRDS = 3
F32 = jnp.float32
BF16 = jnp.bfloat16


def dot(a, b):
    return jnp.dot(a, b, preferred_element_type=F32)


def dot_t(a, b):
    return lax.dot_general(a, b, (((1,), (1,)), ((), ())), preferred_element_type=F32)


def iota(shape, dim):
    return lax.broadcasted_iota(jnp.int32, shape, dim)


def block_of(token):
    return sum((token >= ROWS * k).astype(jnp.int32) for k in range(1, NZ + 1))


def thirds(value):
    high = value.astype(BF16).astype(F32)
    rest = value - high
    middle = rest.astype(BF16).astype(F32)
    return high, middle, rest - middle


def pack_kernel(act, grad, ra1, rb1, ra2, rb2, ga1, gb1, ga2, gb2, out, meta):
    width = act.shape[1]
    out[:, 0:width] = act[...]
    out[:, width : 2 * width] = grad[...]
    meta[...] = jnp.zeros_like(meta)
    arrays = [r[...].astype(F32) for r in (ra1, rb1, ra2, rb2)]
    for g in (ga1, gb1, ga2, gb2):
        arrays.extend(thirds(g[...]))
    for i, block in enumerate(arrays):
        meta[TOP * i : TOP * (i + 1), 0:ROWS] = block
    out[:, 2 * width : 2 * width + LANES] = meta[...].T[0:ROWS].astype(BF16)


def meta_of(pieces):
    parts = [p[...].astype(F32) for p in pieces]
    parts.append(jnp.zeros((LANES - TOKENS, LANES), F32))
    return jnp.concatenate(parts, axis=0).T


def ranks_of(meta, place, i):
    lane = iota((TOP, LANES), 1)
    zpos = place // PLANE
    route = meta[TOP * i : TOP * (i + 1)] - (zpos * PLANE).astype(F32)
    route = jnp.where(lane < TOKENS, route, -1.0)
    expert = iota((PLANE, LANES), 0).astype(F32)
    hits = [(route[j : j + 1, :] == expert).astype(F32) for j in range(TOP)]
    named = sum(hits[1:], hits[0])
    before = iota((LANES, LANES), 0)
    later = iota((LANES, LANES), 1)
    earlier = (block_of(before) == block_of(later)) & (before < later)
    rank = dot(named.astype(BF16), earlier.astype(F32).astype(BF16))
    return named * (rank + 1.0), hits


def select_of(rank):
    row = iota((SLOTS, LANES), 0)
    col = iota((SLOTS, LANES), 1)
    target = jnp.where((row // CAP) % NZ == block_of(col), row % CAP + 1, -1).astype(F32)
    copies = iota((SLOTS, PLANE), 0) // (NZ * CAP) == iota((SLOTS, PLANE), 1)
    spread = dot(copies.astype(F32).astype(BF16), rank.astype(BF16))
    return (spread == target).astype(F32).astype(BF16)


def stack(pieces):
    parts = [p[...].astype(F32) for p in pieces]
    parts.append(jnp.zeros((LANES - TOKENS, parts[0].shape[1]), F32))
    return jnp.concatenate(parts, axis=0).astype(BF16)


def first_kernel(place, m0, m1, m2, m3, p0, p1, p2, p3, out, select):
    @pl.when(pl.program_id(0) == 0)
    def _():
        rank, _ = ranks_of(meta_of((m0, m1, m2, m3)), place[0], 1)
        select[...] = select_of(rank)

    out[...] = dot(select[...], stack((p0, p1, p2, p3))).astype(BF16)


def plan_kernel(place, m0, m1, m2, m3, select, weight):
    meta = meta_of((m0, m1, m2, m3))
    copies = iota((PLANE, SLOTS), 1) // (NZ * CAP) == iota((PLANE, SLOTS), 0)
    copies = copies.astype(F32).astype(BF16)
    row = iota((LANES, SLOTS), 1)
    col = iota((LANES, SLOTS), 0)
    target = jnp.where((row // CAP) % NZ == block_of(col), row % CAP + 1, -1).astype(F32)
    for i in range(4):
        rank, hits = ranks_of(meta, place[0], i)
        if i != 1:
            select[i - i // 2] = select_of(rank)
        mask = dot(rank.T.astype(BF16), copies) == target
        for part in range(3):
            first = TOP * (4 + 3 * i + part)
            gate = meta[first : first + TOP]
            named = sum(hits[j] * gate[j : j + 1, :] for j in range(TOP))
            spread = dot(named.T.astype(BF16), copies)
            weight[i, part] = jnp.where(mask, spread, 0.0).astype(BF16)


def dispatch_kernel(select, p0, p1, p2, p3, out):
    out[...] = dot(select[0], stack((p0, p1, p2, p3))).astype(BF16)


def combine_kernel(weight, rows, own, b1, b2, b3):
    values = rows[...]
    total = sum(dot(weight[0, part], values) for part in range(3))
    own[...] = total[0:ROWS]
    for k, out in ((1, b1), (2, b2), (3, b3)):
        out[...] = total[ROWS * k : ROWS * (k + 1)].astype(BF16)


def sum_of(own, b1, b2, b3):
    total = own[...] + b1[...].astype(F32) + b2[...].astype(F32) + b3[...].astype(F32)
    return total.astype(BF16)


def sum_kernel(own, b1, b2, b3, out):
    out[...] = sum_of(own, b1, b2, b3)


def pass_kernel(edge, own, b1, b2, b3, enter, out, onward):
    total = sum_of(own, b1, b2, b3)
    out[...] = total
    onward[...] = total

    @pl.when(edge[0] == 1)
    def _():
        onward[...] = enter[...]


def part(ref, k):
    size = ref.shape[0] // PIECES
    return ref.at[pl.ds(pl.multiple_of(size * k, size), size)]


def fetch(pair, sems, k):
    source, target = pair
    return pltpu.make_async_copy(part(source, k), part(target, k), sems.at[k])


def column(ref, k):
    size = ref.shape[1] // PIECES
    return ref.at[:, pl.ds(pl.multiple_of(size * k, size), size)]


def loop(body, count=PIECES):
    lax.fori_loop(0, count, lambda k, _: body(k), None)


def begin(whole, pieces, sems, semp):
    for i, (source, target) in enumerate(whole):
        pltpu.make_async_copy(source, target, sems.at[i]).start()
    for k in range(PIECES):
        for i, pair in enumerate(pieces):
            fetch(pair, semp.at[i], k).start()


def pre_activations(x, gate, up, semp, gate_pre, up_pre):
    gate_pre[...] = jnp.zeros_like(gate_pre)
    up_pre[...] = jnp.zeros_like(up_pre)

    def step(k):
        for i, (pair, total) in enumerate(((gate, gate_pre), (up, up_pre))):
            fetch(pair, semp.at[i], k).wait()
            total[...] += dot(column(x, k)[...], part(pair[1], k)[...])

    loop(step)


def send(out, result, sent, k):
    return pltpu.make_async_copy(column(out, k), column(result, k), sent.at[k])


def forward_kernel(rows, w_gate, w_up, w_down, result, *scratch):
    x, gate_mat, up_mat, down_mat, out, gate_pre, up_pre, hidden, sems, semp, sent = scratch
    gate, up = (w_gate, gate_mat), (w_up, up_mat)
    begin(((rows, x),), (gate, up), sems, semp)
    pltpu.make_async_copy(w_down, down_mat, sems.at[1]).start()
    pltpu.make_async_copy(rows, x, sems.at[0]).wait()
    pre_activations(x, gate, up, semp, gate_pre, up_pre)
    hidden[...] = (jax.nn.silu(gate_pre[...]) * up_pre[...]).astype(BF16)
    pltpu.make_async_copy(w_down, down_mat, sems.at[1]).wait()
    target = result.at[:, pl.ds(0, out.shape[1])]

    def step(k):
        column(out, k)[...] = dot(hidden[...], column(down_mat, k)[...]).astype(BF16)
        send(out, target, sent, k).start()

    loop(step)
    for k in range(PIECES):
        send(out, target, sent, k).wait()


def joined_kernel(rows, w_gate, w_up, w_down, extra, result, *scratch):
    held, sem = scratch[-2:]
    width = extra.shape[1]
    into = pltpu.make_async_copy(extra, held, sem.at[0])
    onto = pltpu.make_async_copy(held, result.at[:, pl.ds(width, width)], sem.at[1])
    into.start()
    into.wait()
    onto.start()
    forward_kernel(rows, w_gate, w_up, w_down, result, *scratch[:-2])
    onto.wait()


def backward_kernel(first, second, xs, cs, w_gate, w_up, w_down, result, *scratch):
    x, c, gate_mat, up_mat, down_mat, out = scratch[:6]
    gate_pre, up_pre, d_gate, d_upper, sems, semp, sent = scratch[6:]
    width = x.shape[1]
    gate, up = (w_gate, gate_mat), (w_up, up_mat)
    rows = pltpu.make_async_copy(xs.at[:, pl.ds(first * width, width)], x, sems.at[0])
    cots = pltpu.make_async_copy(cs.at[:, pl.ds(second * width, width)], c, sems.at[1])
    downs = pltpu.make_async_copy(w_down, down_mat, sems.at[2])
    rows.start()
    begin((), (gate, up), sems, semp)
    cots.start()
    downs.start()
    rows.wait()
    pre_activations(x, gate, up, semp, gate_pre, up_pre)
    cots.wait()
    downs.wait()
    size = down_mat.shape[0] // THIRDS

    def inner(k):
        cols = pl.ds(pl.multiple_of(size * k, size), size)
        d_hidden = dot_t(c[...], down_mat[cols, :])
        g, u = gate_pre[:, cols], up_pre[:, cols]
        sigma = jax.nn.sigmoid(g)
        d_gate[:, cols] = (d_hidden * u * sigma * (1.0 + g * (1.0 - sigma))).astype(BF16)
        d_upper[:, cols] = (d_hidden * g * sigma).astype(BF16)

    loop(inner, THIRDS)

    def step(k):
        total = dot_t(d_gate[...], part(gate_mat, k)[...])
        total = total + dot_t(d_upper[...], part(up_mat, k)[...])
        column(out, k)[...] = total.astype(BF16)
        send(out, result, sent, k).start()

    loop(step)
    for k in range(PIECES):
        send(out, result, sent, k).wait()


SMEM = pl.BlockSpec(memory_space=pltpu.SMEM)
ANY = pl.BlockSpec(memory_space=pl.ANY)
HBM = pl.BlockSpec(memory_space=pltpu.HBM)


def spec(shape, index):
    return pl.BlockSpec(shape, index)


def whole(array):
    zeros = (0,) * len(array.shape)
    return pl.BlockSpec(tuple(array.shape), lambda *_: zeros)


def shaped(*shape, dtype=BF16):
    return jax.ShapeDtypeStruct(shape, dtype)


def after(value, *others):
    return lax.optimization_barrier((value,) + others)[0]


def call(
    line, kernel, name, grid, in_specs, args, out_specs, outs, scratch=(), flops=0, room=16
):
    if line:
        args = (after(args[0], line[-1]),) + tuple(args[1:])
    moved = sum(a.size * a.dtype.itemsize for a in args)
    moved += sum(o.size * o.dtype.itemsize for o in outs)
    results = pl.pallas_call(
        kernel,
        name=name,
        grid=grid,
        in_specs=in_specs,
        out_specs=out_specs,
        out_shape=outs,
        scratch_shapes=scratch,
        cost_estimate=pl.CostEstimate(flops=flops, bytes_accessed=moved, transcendentals=0),
        compiler_params=pltpu.CompilerParams(
            vmem_limit_bytes=room << 20, dimension_semantics=("arbitrary",) * len(grid)
        ),
    )(*args)
    line.append(results[0])
    return results


def shift(block, axis, k):
    size = lax.axis_size(axis)
    return lax.ppermute(block, axis, [(i, (i + k) % size) for i in range(size)])


def to_section(block, step, k):
    sections = lax.axis_size("segment")
    route = [
        (s * NZ + i, ((s + step) % sections) * NZ + (i + k) % NZ)
        for s in range(sections)
        for i in range(NZ)
    ]
    return lax.ppermute(block, ("segment", "z"), route)


def gather_z(block):
    return (block,) + tuple(shift(block, "z", k) for k in (1, 2, 3))


def plane(rows):
    block = rows.reshape(PLANE, NZ * CAP, rows.shape[-1])
    return lax.all_to_all(block, ("x", "y"), split_axis=0, concat_axis=0, tiled=True).reshape(
        rows.shape
    )


def shards(
    act_a,
    route_a1,
    gate_a1,
    act_b1,
    route_b1,
    gate_b1,
    grad_b1,
    act_b2,
    route_a2,
    gate_a2,
    route_b2,
    gate_b2,
    enter_a,
    enter_grad,
    w_gate,
    w_up,
    w_down,
):
    width = act_a.shape[2]
    hidden = w_gate.shape[3]
    mats = (w_gate[0, 0], w_up[0, 0], w_down[0, 0])
    place = lax.axis_index(("z", "x", "y")).astype(jnp.int32)[None]
    section = lax.axis_index("segment")
    last = lax.axis_size("segment") - 1
    half = width // 2
    buffer = shaped(SLOTS, width)
    slot_specs = [spec((SLOTS, half), lambda i: (0, i))]
    row_specs = [spec((ROWS, half), lambda i: (0, i))] * NZ

    line = []
    run = functools.partial(call, line)
    args = (act_b1[0], grad_b1[0]) + tuple(
        v[0].T
        for v in (route_a1, route_b1, route_a2, route_b2, gate_a1, gate_b1, gate_a2, gate_b2)
    )
    packed = shaped(ROWS, 2 * width + LANES)
    (head,) = run(
        pack_kernel,
        "pack",
        (1,),
        [whole(a) for a in args],
        args,
        [whole(packed)],
        [packed],
        [pltpu.VMEM((LANES, LANES), F32)],
        room=60,
    )
    head = gather_z(head)
    meta_specs = [spec((ROWS, LANES), lambda i: (0, 2 * width // LANES))] * NZ
    (send_b1,) = run(
        first_kernel,
        "first",
        (4,),
        [SMEM] + meta_specs + row_specs,
        (place,) + head + head,
        slot_specs,
        [shaped(SLOTS, 2 * width)],
        [pltpu.VMEM((SLOTS, LANES), BF16)],
    )
    plans = [shaped(3, SLOTS, LANES), shaped(4, 3, LANES, SLOTS)]
    select, weight = run(
        plan_kernel,
        "plan",
        (1,),
        [SMEM] + meta_specs,
        (place,) + head,
        [whole(p) for p in plans],
        plans,
    )

    def dispatch(i, pieces):
        size = pieces[0].shape[1]
        (rows,) = run(
            dispatch_kernel,
            "dispatch",
            (size // half,),
            [spec((1, SLOTS, LANES), lambda _: (i - i // 2, 0, 0))]
            + [spec((ROWS, half), lambda j: (0, j))] * NZ,
            (select,) + tuple(pieces),
            slot_specs,
            [shaped(SLOTS, size)],
        )
        return rows

    def combine(i, rows):
        parts = run(
            combine_kernel,
            "combine",
            (2,),
            [spec((1, 3, LANES, SLOTS), lambda _: (i, 0, 0, 0))] + slot_specs,
            (weight, rows),
            row_specs,
            [shaped(ROWS, width, dtype=F32)] + [shaped(ROWS, width)] * 3,
        )
        return [parts[0]] + [shift(parts[k], "z", -k) for k in (1, 2, 3)]

    def finish(parts):
        out = shaped(ROWS, width)
        (total,) = run(
            sum_kernel, "sum", (1,), [whole(p) for p in parts], parts, [whole(out)], [out]
        )
        return total

    def onward(parts, edge, enter, step):
        out = shaped(ROWS, width)
        args = (edge.astype(jnp.int32)[None],) + tuple(parts) + (enter,)
        total, moving = run(
            pass_kernel,
            "pass",
            (1,),
            [SMEM] + [whole(a) for a in args[1:]],
            args,
            [whole(out)] * 2,
            [out] * 2,
        )
        return total, [to_section(moving, step, k) for k in range(NZ)]

    rows_buffer = pltpu.VMEM((SLOTS, width), BF16)
    wide_buffer = pltpu.VMEM((SLOTS, hidden), F32)
    thin_buffer = pltpu.VMEM((SLOTS, hidden), BF16)
    mat_buffers = [pltpu.VMEM(m.shape, BF16) for m in mats]

    def forward(rows, *extra):
        (out,) = run(
            joined_kernel if extra else forward_kernel,
            "forward",
            (),
            [ANY] + [HBM] * 3 + [ANY] * len(extra),
            (rows,) + mats + extra,
            [ANY],
            [shaped(SLOTS, width * (1 + len(extra)))],
            [rows_buffer]
            + mat_buffers
            + [
                rows_buffer,
                wide_buffer,
                wide_buffer,
                thin_buffer,
                pltpu.SemaphoreType.DMA((2,)),
                pltpu.SemaphoreType.DMA((2, PIECES)),
                pltpu.SemaphoreType.DMA((PIECES,)),
            ]
            + [rows_buffer, pltpu.SemaphoreType.DMA((2,))] * len(extra),
            6 * SLOTS * width * hidden,
            room=60,
        )
        return out

    def backward(x, c, first, second):
        (out,) = run(
            functools.partial(backward_kernel, first, second),
            "backward",
            (),
            [ANY] * 2 + [HBM] * 3,
            (x, c) + mats,
            [ANY],
            [shaped(SLOTS, width)],
            [rows_buffer, rows_buffer]
            + mat_buffers
            + [
                rows_buffer,
                wide_buffer,
                wide_buffer,
                thin_buffer,
                thin_buffer,
                pltpu.SemaphoreType.DMA((3,)),
                pltpu.SemaphoreType.DMA((2, PIECES)),
                pltpu.SemaphoreType.DMA((PIECES,)),
            ],
            10 * SLOTS * width * hidden,
            room=60,
        )
        return out

    at_b1 = plane(send_b1)
    a_one, x_two = gather_z(after(act_a[0], line[-1])), gather_z(after(act_b2[0], line[-1]))
    send_f1 = dispatch(0, a_one)
    send_x2 = dispatch(3, x_two)
    at_f1 = plane(after(send_f1, at_b1, send_x2))
    back_b1 = plane(after(backward(at_b1, at_b1, 0, 1), at_f1))
    back_f1 = plane(after(forward(at_f1, send_x2), back_b1))
    parts_b = combine(1, back_b1)
    grad_one, cot_two = onward(parts_b, section == 0, enter_grad, -1)
    send_c2 = dispatch(3, cot_two)
    at_c2 = plane(after(send_c2, back_f1))
    parts_f = combine(0, back_f1)
    fwd_one, in_two = onward(parts_f, section == last, enter_a, 1)
    at_f2 = plane(after(dispatch(2, in_two), at_c2))
    back_b2 = plane(after(backward(back_f1, at_c2, 1, 0), at_f2))
    back_f2 = plane(after(forward(at_f2), back_b2))
    grad_two = finish(combine(3, back_b2))
    fwd_two = finish(combine(2, back_f2))
    return fwd_one[None], grad_one[None], fwd_two[None], grad_two[None]


def solution(mesh):
    segments, experts = mesh.devices.shape
    grid = Mesh(
        mesh.devices.reshape(segments, NZ, SIDE, experts // NZ // SIDE),
        ("segment", "z", "x", "y"),
    )
    spread = ("z", "x", "y")
    tokens = P("segment", spread, None)
    weights = P("segment", spread, None, None)
    in_specs = (tokens,) * 12 + (P(spread, None),) * 2 + (weights,) * 3
    return jax.shard_map(
        shards, mesh=grid, in_specs=in_specs, out_specs=(tokens,) * 4, check_vma=False
    )
```

```python
import functools

import jax
import jax.numpy as jnp
from jax import lax
from jax.experimental import pallas as pl
from jax.experimental.pallas import tpu as pltpu
from jax.sharding import Mesh, PartitionSpec as P

TOP = 8
ROWS = 24
NZ = 4
SIDE = 4
PLANE = 16
CAP = 4
SLOTS = PLANE * NZ * CAP
TOKENS = NZ * ROWS
LANES = 128
PIECES = 4
THIRDS = 3
F32 = jnp.float32
BF16 = jnp.bfloat16


def dot(a, b):
    return jnp.dot(a, b, preferred_element_type=F32)


def dot_t(a, b):
    return lax.dot_general(a, b, (((1,), (1,)), ((), ())), preferred_element_type=F32)


def iota(shape, dim):
    return lax.broadcasted_iota(jnp.int32, shape, dim)


def block_of(token):
    return sum((token >= ROWS * k).astype(jnp.int32) for k in range(1, NZ + 1))


def thirds(value):
    high = value.astype(BF16).astype(F32)
    rest = value - high
    middle = rest.astype(BF16).astype(F32)
    return high, middle, rest - middle


def pack_kernel(act, grad, ra1, rb1, ra2, rb2, ga1, gb1, ga2, gb2, out, meta):
    width = act.shape[1]
    out[:, 0:width] = act[...]
    out[:, width : 2 * width] = grad[...]
    meta[...] = jnp.zeros_like(meta)
    arrays = [r[...].astype(F32) for r in (ra1, rb1, ra2, rb2)]
    for g in (ga1, gb1, ga2, gb2):
        arrays.extend(thirds(g[...]))
    for i, block in enumerate(arrays):
        meta[TOP * i : TOP * (i + 1), 0:ROWS] = block
    out[:, 2 * width : 2 * width + LANES] = meta[...].T[0:ROWS].astype(BF16)


def meta_of(pieces):
    parts = [p[...].astype(F32) for p in pieces]
    parts.append(jnp.zeros((LANES - TOKENS, LANES), F32))
    return jnp.concatenate(parts, axis=0).T


def ranks_of(meta, place, i):
    lane = iota((TOP, LANES), 1)
    zpos = place // PLANE
    route = meta[TOP * i : TOP * (i + 1)] - (zpos * PLANE).astype(F32)
    route = jnp.where(lane < TOKENS, route, -1.0)
    expert = iota((PLANE, LANES), 0).astype(F32)
    hits = [(route[j : j + 1, :] == expert).astype(F32) for j in range(TOP)]
    named = sum(hits[1:], hits[0])
    before = iota((LANES, LANES), 0)
    later = iota((LANES, LANES), 1)
    earlier = (block_of(before) == block_of(later)) & (before < later)
    rank = dot(named.astype(BF16), earlier.astype(F32).astype(BF16))
    return named * (rank + 1.0), hits


def select_of(rank):
    row = iota((SLOTS, LANES), 0)
    col = iota((SLOTS, LANES), 1)
    target = jnp.where((row // CAP) % NZ == block_of(col), row % CAP + 1, -1).astype(F32)
    copies = iota((SLOTS, PLANE), 0) // (NZ * CAP) == iota((SLOTS, PLANE), 1)
    spread = dot(copies.astype(F32).astype(BF16), rank.astype(BF16))
    return (spread == target).astype(F32).astype(BF16)


def stack(pieces):
    parts = [p[...].astype(F32) for p in pieces]
    parts.append(jnp.zeros((LANES - TOKENS, parts[0].shape[1]), F32))
    return jnp.concatenate(parts, axis=0).astype(BF16)


def first_kernel(place, m0, m1, m2, m3, p0, p1, p2, p3, out, select):
    @pl.when(pl.program_id(0) == 0)
    def _():
        rank, _ = ranks_of(meta_of((m0, m1, m2, m3)), place[0], 1)
        select[...] = select_of(rank)

    out[...] = dot(select[...], stack((p0, p1, p2, p3))).astype(BF16)


def plan_kernel(place, m0, m1, m2, m3, select, weight):
    meta = meta_of((m0, m1, m2, m3))
    copies = iota((PLANE, SLOTS), 1) // (NZ * CAP) == iota((PLANE, SLOTS), 0)
    copies = copies.astype(F32).astype(BF16)
    row = iota((LANES, SLOTS), 1)
    col = iota((LANES, SLOTS), 0)
    target = jnp.where((row // CAP) % NZ == block_of(col), row % CAP + 1, -1).astype(F32)
    for i in range(4):
        rank, hits = ranks_of(meta, place[0], i)
        if i != 1:
            select[i - i // 2] = select_of(rank)
        mask = dot(rank.T.astype(BF16), copies) == target
        for part in range(3):
            first = TOP * (4 + 3 * i + part)
            gate = meta[first : first + TOP]
            named = sum(hits[j] * gate[j : j + 1, :] for j in range(TOP))
            spread = dot(named.T.astype(BF16), copies)
            weight[i, part] = jnp.where(mask, spread, 0.0).astype(BF16)


def dispatch_kernel(select, p0, p1, p2, p3, out):
    out[...] = dot(select[0], stack((p0, p1, p2, p3))).astype(BF16)


def combine_kernel(weight, rows, own, b1, b2, b3):
    values = rows[...]
    total = sum(dot(weight[0, part], values) for part in range(3))
    own[...] = total[0:ROWS]
    for k, out in ((1, b1), (2, b2), (3, b3)):
        out[...] = total[ROWS * k : ROWS * (k + 1)].astype(BF16)


def sum_of(own, b1, b2, b3):
    total = own[...] + b1[...].astype(F32) + b2[...].astype(F32) + b3[...].astype(F32)
    return total.astype(BF16)


def sum_kernel(own, b1, b2, b3, out):
    out[...] = sum_of(own, b1, b2, b3)


def pass_kernel(edge, own, b1, b2, b3, enter, out, onward):
    total = sum_of(own, b1, b2, b3)
    out[...] = total
    onward[...] = total

    @pl.when(edge[0] == 1)
    def _():
        onward[...] = enter[...]


def part(ref, k):
    size = ref.shape[0] // PIECES
    return ref.at[pl.ds(pl.multiple_of(size * k, size), size)]


def fetch(pair, sems, k):
    source, target = pair
    return pltpu.make_async_copy(part(source, k), part(target, k), sems.at[k])


def column(ref, k):
    size = ref.shape[1] // PIECES
    return ref.at[:, pl.ds(pl.multiple_of(size * k, size), size)]


def loop(body, count=PIECES):
    lax.fori_loop(0, count, lambda k, _: body(k), None)


def begin(whole, pieces, sems, semp):
    for i, (source, target) in enumerate(whole):
        pltpu.make_async_copy(source, target, sems.at[i]).start()
    for k in range(PIECES):
        for i, pair in enumerate(pieces):
            fetch(pair, semp.at[i], k).start()


def pre_activations(x, gate, up, semp, gate_pre, up_pre):
    gate_pre[...] = jnp.zeros_like(gate_pre)
    up_pre[...] = jnp.zeros_like(up_pre)

    def step(k):
        for i, (pair, total) in enumerate(((gate, gate_pre), (up, up_pre))):
            fetch(pair, semp.at[i], k).wait()
            total[...] += dot(column(x, k)[...], part(pair[1], k)[...])

    loop(step)


def send(out, result, sent, k):
    return pltpu.make_async_copy(column(out, k), column(result, k), sent.at[k])


def forward_kernel(rows, w_gate, w_up, w_down, result, *scratch):
    x, gate_mat, up_mat, down_mat, out, gate_pre, up_pre, hidden, sems, semp, sent = scratch
    gate, up = (w_gate, gate_mat), (w_up, up_mat)
    begin(((rows, x),), (gate, up), sems, semp)
    pltpu.make_async_copy(w_down, down_mat, sems.at[1]).start()
    pltpu.make_async_copy(rows, x, sems.at[0]).wait()
    pre_activations(x, gate, up, semp, gate_pre, up_pre)
    hidden[...] = (jax.nn.silu(gate_pre[...]) * up_pre[...]).astype(BF16)
    pltpu.make_async_copy(w_down, down_mat, sems.at[1]).wait()
    target = result.at[:, pl.ds(0, out.shape[1])]

    def step(k):
        column(out, k)[...] = dot(hidden[...], column(down_mat, k)[...]).astype(BF16)
        send(out, target, sent, k).start()

    loop(step)
    for k in range(PIECES):
        send(out, target, sent, k).wait()


def joined_kernel(rows, w_gate, w_up, w_down, extra, result, *scratch):
    held, sem = scratch[-2:]
    width = extra.shape[1]
    into = pltpu.make_async_copy(extra, held, sem.at[0])
    onto = pltpu.make_async_copy(held, result.at[:, pl.ds(width, width)], sem.at[1])
    into.start()
    into.wait()
    onto.start()
    forward_kernel(rows, w_gate, w_up, w_down, result, *scratch[:-2])
    onto.wait()


def backward_kernel(first, second, xs, cs, w_gate, w_up, w_down, result, *scratch):
    x, c, gate_mat, up_mat, down_mat, out = scratch[:6]
    gate_pre, up_pre, d_gate, d_upper, sems, semp, sent = scratch[6:]
    width = x.shape[1]
    gate, up = (w_gate, gate_mat), (w_up, up_mat)
    rows = pltpu.make_async_copy(xs.at[:, pl.ds(first * width, width)], x, sems.at[0])
    cots = pltpu.make_async_copy(cs.at[:, pl.ds(second * width, width)], c, sems.at[1])
    downs = pltpu.make_async_copy(w_down, down_mat, sems.at[2])
    rows.start()
    begin((), (gate, up), sems, semp)
    cots.start()
    downs.start()
    rows.wait()
    pre_activations(x, gate, up, semp, gate_pre, up_pre)
    cots.wait()
    downs.wait()
    size = down_mat.shape[0] // THIRDS

    def inner(k):
        cols = pl.ds(pl.multiple_of(size * k, size), size)
        d_hidden = dot_t(c[...], down_mat[cols, :])
        g, u = gate_pre[:, cols], up_pre[:, cols]
        sigma = jax.nn.sigmoid(g)
        d_gate[:, cols] = (d_hidden * u * sigma * (1.0 + g * (1.0 - sigma))).astype(BF16)
        d_upper[:, cols] = (d_hidden * g * sigma).astype(BF16)

    loop(inner, THIRDS)

    def step(k):
        total = dot_t(d_gate[...], part(gate_mat, k)[...])
        total = total + dot_t(d_upper[...], part(up_mat, k)[...])
        column(out, k)[...] = total.astype(BF16)
        send(out, result, sent, k).start()

    loop(step)
    for k in range(PIECES):
        send(out, result, sent, k).wait()


SMEM = pl.BlockSpec(memory_space=pltpu.SMEM)
ANY = pl.BlockSpec(memory_space=pl.ANY)
HBM = pl.BlockSpec(memory_space=pltpu.HBM)


def spec(shape, index):
    return pl.BlockSpec(shape, index)


def whole(array):
    zeros = (0,) * len(array.shape)
    return pl.BlockSpec(tuple(array.shape), lambda *_: zeros)


def shaped(*shape, dtype=BF16):
    return jax.ShapeDtypeStruct(shape, dtype)


def after(value, *others):
    return lax.optimization_barrier((value,) + others)[0]


def call(
    line, kernel, name, grid, in_specs, args, out_specs, outs, scratch=(), flops=0, room=16
):
    if line:
        args = (after(args[0], line[-1]),) + tuple(args[1:])
    moved = sum(a.size * a.dtype.itemsize for a in args)
    moved += sum(o.size * o.dtype.itemsize for o in outs)
    results = pl.pallas_call(
        kernel,
        name=name,
        grid=grid,
        in_specs=in_specs,
        out_specs=out_specs,
        out_shape=outs,
        scratch_shapes=scratch,
        cost_estimate=pl.CostEstimate(flops=flops, bytes_accessed=moved, transcendentals=0),
        compiler_params=pltpu.CompilerParams(
            vmem_limit_bytes=room << 20, dimension_semantics=("arbitrary",) * len(grid)
        ),
    )(*args)
    line.append(results[0])
    return results


def shift(block, axis, k):
    size = lax.axis_size(axis)
    return lax.ppermute(block, axis, [(i, (i + k) % size) for i in range(size)])


def to_section(block, step, k):
    sections = lax.axis_size("segment")
    route = [
        (s * NZ + i, ((s + step) % sections) * NZ + (i + k) % NZ)
        for s in range(sections)
        for i in range(NZ)
    ]
    return lax.ppermute(block, ("segment", "z"), route)


def gather_z(block):
    return (block,) + tuple(shift(block, "z", k) for k in (1, 2, 3))


def plane(rows):
    block = rows.reshape(PLANE, NZ * CAP, rows.shape[-1])
    return lax.all_to_all(block, ("x", "y"), split_axis=0, concat_axis=0, tiled=True).reshape(
        rows.shape
    )


def shards(
    act_a,
    route_a1,
    gate_a1,
    act_b1,
    route_b1,
    gate_b1,
    grad_b1,
    act_b2,
    route_a2,
    gate_a2,
    route_b2,
    gate_b2,
    enter_a,
    enter_grad,
    w_gate,
    w_up,
    w_down,
):
    width = act_a.shape[2]
    hidden = w_gate.shape[3]
    mats = (w_gate[0, 0], w_up[0, 0], w_down[0, 0])
    place = lax.axis_index(("z", "x", "y")).astype(jnp.int32)[None]
    section = lax.axis_index("segment")
    last = lax.axis_size("segment") - 1
    half = width // 2
    buffer = shaped(SLOTS, width)
    slot_specs = [spec((SLOTS, half), lambda i: (0, i))]
    row_specs = [spec((ROWS, half), lambda i: (0, i))] * NZ

    line = []
    run = functools.partial(call, line)
    args = (act_b1[0], grad_b1[0]) + tuple(
        v[0].T
        for v in (route_a1, route_b1, route_a2, route_b2, gate_a1, gate_b1, gate_a2, gate_b2)
    )
    packed = shaped(ROWS, 2 * width + LANES)
    (head,) = run(
        pack_kernel,
        "pack",
        (1,),
        [whole(a) for a in args],
        args,
        [whole(packed)],
        [packed],
        [pltpu.VMEM((LANES, LANES), F32)],
        room=60,
    )
    head = gather_z(head)
    meta_specs = [spec((ROWS, LANES), lambda i: (0, 2 * width // LANES))] * NZ
    (send_b1,) = run(
        first_kernel,
        "first",
        (4,),
        [SMEM] + meta_specs + row_specs,
        (place,) + head + head,
        slot_specs,
        [shaped(SLOTS, 2 * width)],
        [pltpu.VMEM((SLOTS, LANES), BF16)],
    )
    plans = [shaped(3, SLOTS, LANES), shaped(4, 3, LANES, SLOTS)]
    select, weight = run(
        plan_kernel,
        "plan",
        (1,),
        [SMEM] + meta_specs,
        (place,) + head,
        [whole(p) for p in plans],
        plans,
    )

    def dispatch(i, pieces):
        size = pieces[0].shape[1]
        (rows,) = run(
            dispatch_kernel,
            "dispatch",
            (size // half,),
            [spec((1, SLOTS, LANES), lambda _: (i - i // 2, 0, 0))]
            + [spec((ROWS, half), lambda j: (0, j))] * NZ,
            (select,) + tuple(pieces),
            slot_specs,
            [shaped(SLOTS, size)],
        )
        return rows

    def combine(i, rows):
        parts = run(
            combine_kernel,
            "combine",
            (2,),
            [spec((1, 3, LANES, SLOTS), lambda _: (i, 0, 0, 0))] + slot_specs,
            (weight, rows),
            row_specs,
            [shaped(ROWS, width, dtype=F32)] + [shaped(ROWS, width)] * 3,
        )
        return [parts[0]] + [shift(parts[k], "z", -k) for k in (1, 2, 3)]

    def finish(parts):
        out = shaped(ROWS, width)
        (total,) = run(
            sum_kernel, "sum", (1,), [whole(p) for p in parts], parts, [whole(out)], [out]
        )
        return total

    def onward(parts, edge, enter, step):
        out = shaped(ROWS, width)
        args = (edge.astype(jnp.int32)[None],) + tuple(parts) + (enter,)
        total, moving = run(
            pass_kernel,
            "pass",
            (1,),
            [SMEM] + [whole(a) for a in args[1:]],
            args,
            [whole(out)] * 2,
            [out] * 2,
        )
        return total, [to_section(moving, step, k) for k in range(NZ)]

    rows_buffer = pltpu.VMEM((SLOTS, width), BF16)
    wide_buffer = pltpu.VMEM((SLOTS, hidden), F32)
    thin_buffer = pltpu.VMEM((SLOTS, hidden), BF16)
    mat_buffers = [pltpu.VMEM(m.shape, BF16) for m in mats]

    def forward(rows, *extra):
        (out,) = run(
            joined_kernel if extra else forward_kernel,
            "forward",
            (),
            [ANY] + [HBM] * 3 + [ANY] * len(extra),
            (rows,) + mats + extra,
            [ANY],
            [shaped(SLOTS, width * (1 + len(extra)))],
            [rows_buffer]
            + mat_buffers
            + [
                rows_buffer,
                wide_buffer,
                wide_buffer,
                thin_buffer,
                pltpu.SemaphoreType.DMA((2,)),
                pltpu.SemaphoreType.DMA((2, PIECES)),
                pltpu.SemaphoreType.DMA((PIECES,)),
            ]
            + [rows_buffer, pltpu.SemaphoreType.DMA((2,))] * len(extra),
            6 * SLOTS * width * hidden,
            room=60,
        )
        return out

    def backward(x, c, first, second):
        (out,) = run(
            functools.partial(backward_kernel, first, second),
            "backward",
            (),
            [ANY] * 2 + [HBM] * 3,
            (x, c) + mats,
            [ANY],
            [shaped(SLOTS, width)],
            [rows_buffer, rows_buffer]
            + mat_buffers
            + [
                rows_buffer,
                wide_buffer,
                wide_buffer,
                thin_buffer,
                thin_buffer,
                pltpu.SemaphoreType.DMA((3,)),
                pltpu.SemaphoreType.DMA((2, PIECES)),
                pltpu.SemaphoreType.DMA((PIECES,)),
            ],
            10 * SLOTS * width * hidden,
            room=60,
        )
        return out

    at_b1 = plane(send_b1)
    a_one, x_two = gather_z(after(act_a[0], line[-1])), gather_z(after(act_b2[0], line[-1]))
    send_f1 = dispatch(0, a_one)
    send_x2 = dispatch(3, x_two)
    at_f1 = plane(after(send_f1, at_b1, send_x2))
    back_b1 = plane(after(backward(at_b1, at_b1, 0, 1), at_f1))
    out_f1 = forward(at_f1, send_x2)
    parts_b = combine(1, back_b1)
    back_f1 = plane(after(out_f1, parts_b[0]))
    grad_one, cot_two = onward(parts_b, section == 0, enter_grad, -1)
    send_c2 = dispatch(3, cot_two)
    at_c2 = plane(after(send_c2, back_f1))
    parts_f = combine(0, back_f1)
    fwd_one, in_two = onward(parts_f, section == last, enter_a, 1)
    at_f2 = plane(after(dispatch(2, in_two), at_c2))
    back_b2 = plane(after(backward(back_f1, at_c2, 1, 0), at_f2))
    back_f2 = plane(after(forward(at_f2), back_b2))
    grad_two = finish(combine(3, back_b2))
    fwd_two = finish(combine(2, back_f2))
    return fwd_one[None], grad_one[None], fwd_two[None], grad_two[None]


def solution(mesh):
    segments, experts = mesh.devices.shape
    grid = Mesh(
        mesh.devices.reshape(segments, NZ, SIDE, experts // NZ // SIDE),
        ("segment", "z", "x", "y"),
    )
    spread = ("z", "x", "y")
    tokens = P("segment", spread, None)
    weights = P("segment", spread, None, None)
    in_specs = (tokens,) * 12 + (P(spread, None),) * 2 + (weights,) * 3
    return jax.shard_map(
        shards, mesh=grid, in_specs=in_specs, out_specs=(tokens,) * 4, check_vma=False
    )
```
